32 devices in a mesh: seq: 16 (over z, y, x), head: 2 (over core).
Axes of the slice: x: 2, y: 2, z: 4, core: 2. Of those that a mesh axis runs over, the one named last changes fastest.
Arguments:
- queries: bfloat16 [6144, 4096], P('seq', 'head'), may hold values from -32 to 32
- keys: bfloat16 [6144, 1024], P('seq', 'head'), may hold values from -9 to 9
- values: bfloat16 [6144, 1024], P('seq', 'head'), may hold values from -96 to 96
- block_ids: int32 [16, 32, 3], P('seq', 'head'), may hold values from 0 to 15, as said below
- out_weight: bfloat16 [4096, 4096], P('head'), may hold values from -0.09375 to 0.09375
Outputs:
- projected: bfloat16 [4096, 6144], P('head', 'seq')
The draws below stay inside these ranges and needn't reach their ends.
Inputs may be any that keep to these rules, and one draw needn't show every extreme that they name: `block_ids`: for each query block and key/value head, the 12 ids of the query heads that share that key/value head are all different. An id at or above its own query block's index names a block that the causal rule removes.
All inputs are finite; a program needn't handle non-finite values.
Results may differ from the reference program's by a relative error of at most 0.02.
Values may be sent and summed in bfloat16 or wider, within the bound.
A program may use at most 128 MiB of HBM per device.

```python
import math
import jax
import jax.numpy as jnp
from jax import lax

D = 4096
QUERY_HEADS = 32
KEY_VALUE_HEADS = 8
HEAD_DIMENSION = 128
BLOCK_TOKENS = 384
TOPK = 3
QUERY_PER_KEY = 4
BLOCK_COUNT = 16
SEQUENCE_TOKENS = 6144
N_HEAD = 2


def sampled_keys(key):
    random_seed_key = jax.random.fold_in(key, 11)
    raw_logits = jnp.clip(jax.random.normal(random_seed_key, (SEQUENCE_TOKENS, KEY_VALUE_HEADS * HEAD_DIMENSION), jnp.float32), -4.0, 4.0)
    return raw_logits


def draw_keys(key, part):
    return sampled_keys(key).astype(jnp.bfloat16)


def draw_queries(key, part):
    random_seed_key = jax.random.fold_in(key, 21)
    raw_logits = jnp.clip(jax.random.normal(random_seed_key, (SEQUENCE_TOKENS, QUERY_HEADS * HEAD_DIMENSION), jnp.float32), -4.0, 4.0)
    return raw_logits.astype(jnp.bfloat16)


def draw_block_ids(key, part):
    picked_block_index = QUERY_PER_KEY * TOPK
    block_scores = jax.random.randint(jax.random.fold_in(key, 31), (BLOCK_COUNT, KEY_VALUE_HEADS, BLOCK_COUNT), 0, 1024)
    hot = jax.random.randint(jax.random.fold_in(key, 32), (BLOCK_COUNT,), 0, 8) == 0
    blocks = jnp.arange(BLOCK_COUNT, dtype=jnp.int32)
    earlier = blocks[None, None, :] < blocks[:, None, None]
    ranked = jnp.where(earlier, (block_scores + jnp.where(hot, 1024, 0)[None, None, :]) * BLOCK_COUNT + blocks[None, None, :], -1 - blocks[None, None, :])
    first_pick = (blocks[:, None, None] == BLOCK_COUNT - 1) & (blocks[None, None, :] == 0)
    ranked = jnp.where(first_pick, 4096 * BLOCK_COUNT, ranked)
    unused, picked = lax.top_k(ranked, picked_block_index)
    permute_rows = jax.random.randint(jax.random.fold_in(key, 33), (BLOCK_COUNT, KEY_VALUE_HEADS, picked_block_index), 0, 4096) * picked_block_index + jnp.arange(picked_block_index, dtype=jnp.int32)
    order = jnp.argsort(permute_rows, axis=-1)
    picked = jnp.take_along_axis(picked, order, axis=-1)
    return picked.reshape(BLOCK_COUNT, QUERY_HEADS, TOPK).astype(jnp.int32)


def level_of(key, extent, split, least, top_value):
    def one(axis_at, shards_of):
        draws = jax.random.uniform(jax.random.fold_in(jax.random.fold_in(key, 6), axis_at), (shards_of,), jnp.float32, least / len(split), top_value / len(split))
        return jnp.repeat(jnp.exp(draws), extent[axis_at] // shards_of).reshape((-1,) + (1,) * (len(extent) - axis_at - 1))

    gain = one(*split[0])
    for cut in split[1:]:
        gain = gain * one(*cut)
    return gain


def scatter_about(rng, dims, deviation, bound, cuts=(), kind=jnp.bfloat16):
    drawn = jax.random.normal(rng, dims, jnp.float32) * deviation
    if len(cuts) > 0:
        drawn = level_of(rng, dims, cuts, -0.22, 0.18) * drawn
    return jnp.clip(drawn, min=-bound, max=bound).astype(kind)


def setup_inputs(seed: int = 0) -> dict:
    key_list = jax.random.split(jax.random.key(seed), 6)
    return {
        "queries": draw_queries(jax.random.fold_in(key_list[5], 71), 0),
        "keys": draw_keys(jax.random.fold_in(key_list[5], 71), 0),
        "values": scatter_about(key_list[2], (SEQUENCE_TOKENS, KEY_VALUE_HEADS * HEAD_DIMENSION), 16.0, 96.0, ((0, 16), (1, 2))),
        "block_ids": draw_block_ids(jax.random.fold_in(key_list[5], 71), 0),
        "out_weight": scatter_about(key_list[4], (QUERY_HEADS * HEAD_DIMENSION, D), (QUERY_HEADS * HEAD_DIMENSION) ** -0.5, 0.09375, ((0, 2),)),
    }


def block_part(query_tile, key_tile, value_tile, keep):
    block_scores = jnp.einsum('hqd,hkd->hqk', query_tile.astype(jnp.float32), key_tile.astype(jnp.float32)) * (1.0 / math.sqrt(HEAD_DIMENSION))
    if keep is not None:
        block_scores = jnp.where(keep, block_scores, -1e+30)
    top = lax.optimization_barrier(jnp.max(block_scores, axis=-1))
    prob = jnp.exp(block_scores - top[..., None])
    if keep is not None:
        prob = jnp.where(keep, prob, 0.0)
    total = lax.optimization_barrier(jnp.sum(prob, axis=-1))
    rounded = lax.optimization_barrier(prob.astype(jnp.bfloat16))
    part = jnp.einsum('hqk,hkd->hqd', rounded.astype(jnp.float32), value_tile.astype(jnp.float32)).astype(jnp.bfloat16)
    return (part, top, total)

def reference(queries, keys, values, block_ids, out_weight):
    q_blocks = queries.reshape(BLOCK_COUNT, BLOCK_TOKENS, QUERY_HEADS, HEAD_DIMENSION)
    key_block_tiles = keys.reshape(BLOCK_COUNT, BLOCK_TOKENS, KEY_VALUE_HEADS, HEAD_DIMENSION).transpose(0, 2, 1, 3)
    value_block_tiles = values.reshape(BLOCK_COUNT, BLOCK_TOKENS, KEY_VALUE_HEADS, HEAD_DIMENSION).transpose(0, 2, 1, 3)
    head_kv = jnp.arange(QUERY_HEADS, dtype=jnp.int32) // QUERY_PER_KEY
    position = jnp.arange(BLOCK_TOKENS, dtype=jnp.int32)
    causal = position[:, None] >= position[None, :]
    weight_groups = out_weight.reshape(N_HEAD, QUERY_HEADS * HEAD_DIMENSION // N_HEAD, D).astype(jnp.float32)

    def one_block(index):
        query_rows = q_blocks[index].transpose(1, 0, 2)
        own_part, own_top, own_total = block_part(query_rows, key_block_tiles[index][head_kv], value_block_tiles[index][head_kv], causal[None])
        chosen = block_ids[index]
        live = chosen < index
        k_sel = key_block_tiles[chosen, head_kv[:, None]].reshape(QUERY_HEADS * TOPK, BLOCK_TOKENS, HEAD_DIMENSION)
        v_sel = value_block_tiles[chosen, head_kv[:, None]].reshape(QUERY_HEADS * TOPK, BLOCK_TOKENS, HEAD_DIMENSION)
        repeated = jnp.repeat(query_rows, TOPK, axis=0)
        sel_part, sel_top, sel_total = block_part(repeated, k_sel, v_sel, None)
        sel_part = sel_part.reshape(QUERY_HEADS, TOPK, BLOCK_TOKENS, HEAD_DIMENSION)
        sel_top = sel_top.reshape(QUERY_HEADS, TOPK, BLOCK_TOKENS)
        sel_total = sel_total.reshape(QUERY_HEADS, TOPK, BLOCK_TOKENS)
        safe_top = jnp.where(live[..., None], sel_top, own_top[:, None, :])
        top = jnp.maximum(own_top, lax.optimization_barrier(jnp.max(safe_top, axis=1)))
        own_weight = jnp.exp(own_top - top)
        sel_weight = jnp.where(live[..., None], jnp.exp(safe_top - top[:, None, :]), 0.0)
        total = own_weight * own_total + lax.optimization_barrier(jnp.sum(sel_weight * sel_total, axis=1))
        accum = own_weight[..., None] * own_part.astype(jnp.float32) + lax.optimization_barrier(jnp.sum(sel_weight[..., None] * sel_part.astype(jnp.float32), axis=1))
        attended = (accum / total[..., None]).transpose(1, 0, 2).reshape(BLOCK_TOKENS, QUERY_HEADS * HEAD_DIMENSION).astype(jnp.bfloat16)
        grouped = attended.reshape(BLOCK_TOKENS, N_HEAD, QUERY_HEADS * HEAD_DIMENSION // N_HEAD).astype(jnp.float32)
        pieces = jnp.einsum('tnf,nfd->ntd', grouped, weight_groups).astype(jnp.bfloat16)
        pieces = lax.optimization_barrier(pieces)
        return lax.optimization_barrier(jnp.sum(pieces.astype(jnp.float32), axis=0)).astype(jnp.bfloat16)
    mixed = lax.map(one_block, jnp.arange(BLOCK_COUNT, dtype=jnp.int32))
    return mixed.reshape(SEQUENCE_TOKENS, D).T
```

```python
import functools
import math

import jax
import jax.numpy as jnp
from jax import lax
from jax.experimental import pallas as pl
from jax.experimental.pallas import tpu as pltpu
from jax.sharding import PartitionSpec as P

HEAD_DIMENSION = 128
MESH = pl.DeviceIdType.MESH
LOW = -1e30


def member(position, step, size):
    if size & (size - 1):
        return lax.rem(step - position + size, size)
    other, bit = 0, 1
    while bit < size:
        digit = (position // bit) % 2
        other = other + bit * ((digit + (step // bit) % 2) % 2)
        bit *= 2
    return other


def attend(k, q, v_t, factor, keep):
    scores = lax.dot_general(k, q, (((1,), (1,)), ((), ())), preferred_element_type=jnp.float32)
    if keep is not None:
        scores = jnp.where(keep, scores, LOW)
    top = jnp.max(scores, axis=0, keepdims=True)
    prob = jnp.exp2((scores - top) * factor)
    total = jnp.sum(prob, axis=0, keepdims=True)
    part = jnp.dot(v_t, prob.astype(jnp.bfloat16), preferred_element_type=jnp.float32)
    return part.astype(jnp.bfloat16), top, total


def kernel(
    dims,
    ids_hbm, q_hbm, k_hbm, v_ref, w_hbm,
    out_ref,
    kbuf, vbuf, parts, stats, own_parts, own_stats, wbuf,
    att_out, att_in, piece_out, piece_in, v_own, ids_in, ids, table, acc,
    k_recv, v_recv, k_fwd, v_fwd, k_send, v_send, q_send, q_recv,
    att_send, att_recv, piece_send, piece_recv, w_sem,
    ids_send, ids_recv, ids_sem, kv_gate, q_gate, chain_gate, *qbuf,
):
    seq_size, head_size, group_size, heads, topk, tile = dims
    rows = k_hbm.shape[0]
    hd = HEAD_DIMENSION
    chains = seq_size // group_size
    width = heads * hd
    me = lax.axis_index("seq")
    mine = lax.axis_index("head")
    plane = me // group_size
    place = me % group_size
    base = plane * group_size
    factor = math.log2(math.e) / math.sqrt(hd)
    others = [member(place, r, group_size) for r in range(group_size)]
    peers = [lax.rem(mine + h, head_size) for h in range(head_size)]
    has_next = plane < chains - 1
    has_prev = plane > 0
    ahead = me + group_size
    stagger = head_size == 2 and group_size > 1
    leads = mine == 0 if stagger else mine >= 0
    trails = mine == 1 if stagger else mine < 0

    w_copy = pltpu.make_async_copy(w_hbm, wbuf, w_sem)
    w_copy.start()

    barrier = pltpu.get_barrier_semaphore()
    for r in range(1, group_size):
        pl.semaphore_signal(barrier, inc=1, device_id={"seq": base + others[r]}, device_id_type=MESH)
    for h in range(1, head_size):
        pl.semaphore_signal(barrier, inc=1, device_id={"head": peers[h]}, device_id_type=MESH)

    @pl.when(has_next)
    def _():
        pl.semaphore_signal(barrier, inc=1, device_id={"seq": ahead}, device_id_type=MESH)

    @pl.when(has_prev)
    def _():
        pl.semaphore_signal(barrier, inc=1, device_id={"seq": me - group_size}, device_id_type=MESH)

    for g in range(group_size):
        v_own[g] = v_ref[:, g * hd:(g + 1) * hd].T
    near_count = jnp.where(has_next, 1, 0) + jnp.where(has_prev, 1, 0)
    pl.semaphore_wait(barrier, group_size + head_size - 2 + near_count)

    def k_piece(head):
        return k_hbm.at[:, pl.ds(pl.multiple_of(head * hd, hd), hd)]

    def v_piece(head):
        return v_own.at[head]

    def q_piece(head, i):
        return q_hbm.at[:, pl.ds(pl.multiple_of((head * heads + i) * hd, hd), hd)]

    def forward(a, k_src, v_src):
        return (
            pltpu.make_async_remote_copy(
                src_ref=k_src, dst_ref=kbuf.at[a], send_sem=k_fwd.at[a], recv_sem=k_recv.at[a],
                device_id={"seq": ahead}, device_id_type=MESH),
            pltpu.make_async_remote_copy(
                src_ref=v_src, dst_ref=vbuf.at[a], send_sem=v_fwd.at[a], recv_sem=v_recv.at[a],
                device_id={"seq": ahead}, device_id_type=MESH),
        )

    def relay(a):
        return forward(a, kbuf.at[a], vbuf.at[a])

    def to_member(r):
        t = others[r]
        kv = (
            pltpu.make_async_remote_copy(
                src_ref=k_piece(t), dst_ref=kbuf.at[me], send_sem=k_send.at[r], recv_sem=k_recv.at[me],
                device_id={"seq": base + t}, device_id_type=MESH),
            pltpu.make_async_remote_copy(
                src_ref=v_piece(t), dst_ref=vbuf.at[me], send_sem=v_send.at[r], recv_sem=v_recv.at[me],
                device_id={"seq": base + t}, device_id_type=MESH),
        )
        qs = [
            pltpu.make_async_remote_copy(
                src_ref=q_piece(t, i), dst_ref=qbuf[r].at[i], send_sem=q_send.at[r, i],
                recv_sem=q_recv.at[r, i], device_id={"seq": base + t}, device_id_type=MESH)
            for i in range(heads)
        ]
        return kv, qs

    def ids_copy(r):
        return pltpu.make_async_remote_copy(
            src_ref=ids_hbm, dst_ref=ids_in.at[r], send_sem=ids_send.at[r],
            recv_sem=ids_recv.at[r], device_id={"seq": base + others[r]}, device_id_type=MESH)

    def arrived(a):
        k_copy, v_copy = relay(a)
        k_copy.wait_recv()
        v_copy.wait_recv()

    def pass_on(a):
        @pl.when(has_next)
        def _():
            for copy in relay(a):
                copy.start()

    def open_gate(gate):
        if stagger:
            pl.semaphore_signal(gate, inc=1, device_id={"head": peers[1]}, device_id_type=MESH)

    ids_own = pltpu.make_async_copy(ids_hbm, ids_in.at[0], ids_send.at[0])
    ids_own.start()
    for r in range(1, group_size):
        ids_copy(r).start()
    sends = [None] + [to_member(r) for r in range(1, group_size)]
    own_first = forward(me, k_piece(place), v_piece(place))

    def send_own():
        @pl.when(has_next)
        def _():
            for copy in own_first:
                copy.start()

    def send_keys():
        for r in range(1, group_size):
            for copy in sends[r][0]:
                copy.start()

    def send_queries():
        for r in range(1, group_size):
            for copy in sends[r][1]:
                copy.start()

    send_own()

    @pl.when(leads)
    def _():
        send_keys()

    local = [
        pltpu.make_async_copy(k_piece(place), kbuf.at[me], k_send.at[0]),
        pltpu.make_async_copy(v_piece(place), vbuf.at[me], v_send.at[0]),
    ] + [pltpu.make_async_copy(q_piece(place, i), qbuf[0].at[i], q_send.at[0, i]) for i in range(heads)]
    for copy in local:
        copy.start()

    @pl.when(leads)
    def _():
        send_queries()

    for r in range(group_size):
        parts[r, seq_size] = jnp.zeros((hd, rows), jnp.bfloat16)
        stats[r, seq_size, 0:1, :] = jnp.full((1, rows), LOW, jnp.float32)
        stats[r, seq_size, 1:2, :] = jnp.zeros((1, rows), jnp.float32)
    for copy in local:
        copy.wait()

    causal = lax.broadcasted_iota(jnp.int32, (rows, rows), 0) <= lax.broadcasted_iota(
        jnp.int32, (rows, rows), 1)

    def diagonal(r):
        a = base + others[r]
        keep = jnp.concatenate([causal] * heads, axis=1)
        q = jnp.concatenate([qbuf[r][i] for i in range(heads)], axis=0)
        part, top, total = attend(kbuf[a], q, vbuf[a], factor, keep)
        for i in range(heads):
            span = slice(i * rows, (i + 1) * rows)
            own_parts[r, i] = part[:, span]
            own_stats[r, i, 0:1, :] = top[:, span]
            own_stats[r, i, 1:2, :] = total[:, span]

    def selected(members, a):
        q = jnp.concatenate([qbuf[r][table[r, a]] for r in members], axis=0)
        part, top, total = attend(kbuf[a], q, vbuf[a], factor, None)
        for n, r in enumerate(members):
            span = slice(n * rows, (n + 1) * rows)
            parts[r, a] = part[:, span]
            stats[r, a, 0:1, :] = top[:, span]
            stats[r, a, 1:2, :] = total[:, span]

    def block_at(t):
        level = t // group_size
        return base - (level + 1) * group_size + member(place, t % group_size, group_size)

    def inside(r, first):
        @pl.when(others[first] < others[r])
        def _():
            selected([r], base + others[first])

    def move(t):
        arrived(block_at(t))
        pass_on(block_at(t))

    diagonal(0)
    ids_own.wait()
    for r in range(1, group_size):
        ids_copy(r).wait_recv()
    ids_local = pltpu.make_async_copy(ids_in, ids, ids_sem)
    ids_local.start()
    ids_local.wait()

    picks = [(i, j) for i in range(heads) for j in range(topk)]

    def pick(r, i, j):
        return ids[r, j, 0, place * heads + i]

    def note(a, carry):
        for r in range(group_size):
            head = 0
            for i, j in picks:
                head = jnp.where(pick(r, i, j) == a, i, head)
            table[r, a] = head
        return carry

    @pl.when(trails)
    def _():
        if stagger:
            pl.semaphore_wait(kv_gate, 1)
        send_keys()

    lax.fori_loop(0, base + group_size, note, 0)

    for r in range(1, group_size):
        arrived(base + others[r])

        @pl.when(leads)
        def _():
            pass_on(base + others[r])

    @pl.when(leads)
    def _():
        open_gate(kv_gate)

    for r in range(1, group_size):
        inside(0, r)

    @pl.when(trails)
    def _():
        if stagger:
            pl.semaphore_wait(q_gate, 1)
        send_queries()

    @pl.when(leads & has_prev)
    def _():
        for t in range(group_size):
            move(t)

    def begin_chain():
        if stagger:
            pl.semaphore_wait(chain_gate, 1)
        for r in range(1, group_size):
            pass_on(base + others[r])

    soon = plane < 2
    levels_two = plane > 1

    @pl.when(trails & has_next & soon)
    def _():
        begin_chain()

    @pl.when(leads & has_next & (plane == 0))
    def _():
        open_gate(chain_gate)

    for r in range(1, group_size):
        if r == group_size - 1:
            @pl.when(trails & has_next & jnp.logical_not(soon))
            def _():
                begin_chain()
        for copy in sends[r][1]:
            copy.wait_recv()
        if r == 1:
            @pl.when(leads)
            def _():
                open_gate(q_gate)
        diagonal(r)

    @pl.when(leads & has_next & (plane == 1))
    def _():
        open_gate(chain_gate)

    for r in range(1, group_size):
        for first in range(group_size):
            if first != r:
                inside(r, first)

    def far(t, carry):
        selected(range(group_size), block_at(t))
        return carry

    def far_move(t, carry):
        move(t)
        return far(t, carry)

    def near(t, carry):
        @pl.when(levels_two)
        def _():
            move(t + group_size)
        return far(t, carry)

    @pl.when(leads & has_prev)
    def _():
        lax.fori_loop(0, group_size, near, 0)

    @pl.when(leads & has_next & (plane == 2))
    def _():
        open_gate(chain_gate)

    @pl.when(leads & levels_two)
    def _():
        lax.fori_loop(group_size, 2 * group_size, far, 0)
        lax.fori_loop(2 * group_size, plane * group_size, far_move, 0)

    @pl.when(trails)
    def _():
        lax.fori_loop(0, plane * group_size, far_move, 0)

    @pl.when(leads & has_next & (plane > 2))
    def _():
        open_gate(chain_gate)

    def att_copy(r, i):
        return pltpu.make_async_remote_copy(
            src_ref=att_out.at[r, i], dst_ref=att_in.at[place, i], send_sem=att_send.at[r, i],
            recv_sem=att_recv.at[r, i], device_id={"seq": base + others[r]}, device_id_type=MESH)

    direct = [r for r in range(1, group_size) if not r & (r - 1)]
    through = [r for r in range(1, group_size) if r & (r - 1)] + [0]
    steps = [(r, i) for i in range(heads) for r in direct] + [(r, i) for r in through for i in range(heads)]
    for r, i in steps:
        block = base + others[r]
        tops = [own_stats[r, i, 0:1, :]]
        totals = [own_stats[r, i, 1:2, :]]
        slots = [jnp.where(pick(r, i, j) < block, pick(r, i, j), seq_size) for j in range(topk)]
        for slot in slots:
            tops.append(stats[r, slot, 0:1, :])
            totals.append(stats[r, slot, 1:2, :])
        top = functools.reduce(jnp.maximum, tops)
        weights = [jnp.exp2((one - top) * factor) for one in tops]
        inverse = 1.0 / sum(w * t for w, t in zip(weights, totals))
        weights = [w * inverse for w in weights]
        accum = weights[0] * own_parts[r, i].astype(jnp.float32)
        for slot, weight in zip(slots, weights[1:]):
            accum = accum + weight * parts[r, slot].astype(jnp.float32)
        attended = accum.astype(jnp.bfloat16).T
        if r:
            att_out[r, i] = attended
        else:
            att_in[place, i] = attended
        if r:
            att_copy(r, i).start()

    features = w_hbm.shape[1] // head_size
    tiles = features // tile

    def product(r, start):
        row = pl.multiple_of(others[r] * width, width)
        rows_in = jnp.concatenate([att_in[others[r], i] for i in range(heads)], axis=1)
        return jnp.dot(
            rows_in, wbuf[pl.ds(row, width), pl.ds(start, tile)],
            preferred_element_type=jnp.float32)

    w_copy.wait()

    def share(early, members):
        for r in members:
            if r:
                for i in range(heads):
                    att_copy(r, i).wait_recv()

        def one(n, carry):
            terms = [product(r, pl.multiple_of(n * tile, tile)) for r in members]
            acc[n] = sum(terms) if early else acc[n] + sum(terms)
            return carry

        if members:
            lax.fori_loop(0, head_size * tiles, one, 0)

    share(True, list(range(min(1, group_size - 1))))
    share(False, list(range(1, group_size - 1)))
    if group_size > 1:
        for i in range(heads):
            att_copy(group_size - 1, i).wait_recv()

    def project(peer, n):
        result = product(group_size - 1, pl.multiple_of(peer * features + n * tile, tile))
        if group_size > 1:
            result = result + acc[peer * tiles + n]
        return result.astype(jnp.bfloat16)

    def piece_copy(h, n):
        return pltpu.make_async_remote_copy(
            src_ref=piece_out.at[h - 1, n], dst_ref=piece_in.at[h - 1, n],
            send_sem=piece_send.at[h - 1, n], recv_sem=piece_recv.at[h - 1, n],
            device_id={"head": peers[h]}, device_id_type=MESH)

    for h in range(1, head_size):
        def give(n, carry):
            piece_out[h - 1, n] = project(peers[h], n)
            piece_copy(h, n).start()
            return carry
        lax.fori_loop(0, tiles, give, 0)

    def finish(n, carry):
        total = project(mine, n).astype(jnp.float32)
        for h in range(1, head_size):
            piece_copy(h, n).wait_recv()
            total = total + piece_in[h - 1, n].astype(jnp.float32)
        out_ref[n] = total.astype(jnp.bfloat16)
        return carry

    lax.fori_loop(0, tiles, finish, 0)

    for h in range(1, head_size):
        for n in range(tiles):
            piece_copy(h, n).wait_send()
    for r in range(1, group_size):
        ids_copy(r).wait_send()
        for i in range(heads):
            att_copy(r, i).wait_send()
        for copy in sends[r][0]:
            copy.wait_send()
        for copy in sends[r][1]:
            copy.wait_send()

    @pl.when(has_next)
    def _():
        def gone(a, carry):
            for copy in relay(a):
                copy.wait_send()
            return carry
        lax.fori_loop(0, base + group_size, gone, 0)


def flip(x_ref, out_ref):
    out_ref[...] = x_ref[0].T


def local(seq_size, head_size, queries, keys, values, block_ids, out_weight):
    rows = queries.shape[0]
    hd = HEAD_DIMENSION
    kv_heads = keys.shape[1] // hd
    heads = queries.shape[1] // hd // kv_heads
    topk = block_ids.shape[2]
    model = out_weight.shape[1]
    features = model // head_size
    tile = min(1024, features)
    ids = jnp.transpose(block_ids, (2, 0, 1))
    bf16, f32 = jnp.bfloat16, jnp.float32
    tiles = features // tile
    dma = pltpu.SemaphoreType.DMA
    g = kv_heads
    hbm = pl.BlockSpec(memory_space=pl.ANY)
    more = max(head_size - 1, 1)
    result = pl.pallas_call(
        functools.partial(kernel, (seq_size, head_size, g, heads, topk, tile)),
        out_shape=jax.ShapeDtypeStruct((tiles, rows, tile), bf16),
        in_specs=[hbm, hbm, hbm, pl.BlockSpec(memory_space=pltpu.VMEM), hbm],
        out_specs=pl.BlockSpec(memory_space=pltpu.VMEM),
        scratch_shapes=[
            pltpu.VMEM((seq_size, rows, hd), bf16),
            pltpu.VMEM((seq_size, hd, rows), bf16),
            pltpu.VMEM((g, seq_size + 1, hd, rows), bf16),
            pltpu.VMEM((g, seq_size + 1, 8, rows), f32),
            pltpu.VMEM((g, heads, hd, rows), bf16),
            pltpu.VMEM((g, heads, 8, rows), f32),
            pltpu.VMEM(out_weight.shape, bf16),
            pltpu.VMEM((g, heads, rows, hd), bf16),
            pltpu.VMEM((g, heads, rows, hd), bf16),
            pltpu.VMEM((more, tiles, rows, tile), bf16),
            pltpu.VMEM((more, tiles, rows, tile), bf16),
            pltpu.VMEM((g, hd, rows), bf16),
            pltpu.VMEM((g, *ids.shape), jnp.int32),
            pltpu.SMEM((g, *ids.shape), jnp.int32),
            pltpu.SMEM((g, seq_size), jnp.int32),
            pltpu.VMEM((head_size * tiles, rows, tile), f32),
            dma((seq_size,)), dma((seq_size,)), dma((seq_size,)), dma((seq_size,)),
            dma((g,)), dma((g,)), dma((g, heads)), dma((g, heads)),
            dma((g, heads)), dma((g, heads)), dma((more, tiles)), dma((more, tiles)), dma,
            dma((g,)), dma((g,)), dma,
        ] + [pltpu.SemaphoreType.REGULAR] * 3 + [pltpu.VMEM((heads, rows, hd), bf16)] * g,
        compiler_params=pltpu.CompilerParams(
            collective_id=0, has_side_effects=True, vmem_limit_bytes=60 << 20),
    )(ids, queries, keys, values, out_weight)
    return pl.pallas_call(
        flip,
        grid=(tiles,),
        out_shape=jax.ShapeDtypeStruct((features, rows), bf16),
        in_specs=[pl.BlockSpec((1, rows, tile), lambda n: (n, 0, 0))],
        out_specs=pl.BlockSpec((tile, rows), lambda n: (n, 0)),
    )(result)


def solution(mesh):
    return jax.shard_map(
        functools.partial(local, mesh.shape["seq"], mesh.shape["head"]),
        mesh=mesh,
        in_specs=(
            P("seq", "head"),
            P("seq", "head"),
            P("seq", "head"),
            P("seq", "head", None),
            P("head", None),
        ),
        out_specs=P("head", "seq"),
        check_vma=False,
    )
```

```python
import functools
import math

import jax
import jax.numpy as jnp
from jax import lax
from jax.experimental import pallas as pl
from jax.experimental.pallas import tpu as pltpu
from jax.sharding import PartitionSpec as P

HEAD_DIMENSION = 128
MESH = pl.DeviceIdType.MESH
LOW = -1e30


def member(position, step, size):
    if size & (size - 1):
        return lax.rem(step - position + size, size)
    other, bit = 0, 1
    while bit < size:
        digit = (position // bit) % 2
        other = other + bit * ((digit + (step // bit) % 2) % 2)
        bit *= 2
    return other


def attend(k, q, v_t, factor, keep):
    scores = lax.dot_general(k, q, (((1,), (1,)), ((), ())), preferred_element_type=jnp.float32)
    if keep is not None:
        scores = jnp.where(keep, scores, LOW)
    top = jnp.max(scores, axis=0, keepdims=True)
    prob = jnp.exp2((scores - top) * factor)
    total = jnp.sum(prob, axis=0, keepdims=True)
    part = jnp.dot(v_t, prob.astype(jnp.bfloat16), preferred_element_type=jnp.float32)
    return part.astype(jnp.bfloat16), top, total


def kernel(
    dims,
    ids_hbm, q_hbm, k_hbm, v_ref, w_hbm,
    out_ref,
    kbuf, vbuf, parts, stats, own_parts, own_stats, wbuf,
    att_out, att_in, piece_out, piece_in, v_own, ids_in, ids, table, acc,
    k_recv, v_recv, k_fwd, v_fwd, k_send, v_send, q_send, q_recv,
    att_send, att_recv, piece_send, piece_recv, w_sem,
    ids_send, ids_recv, ids_sem, kv_gate, q_gate, chain_gate, *qbuf,
):
    seq_size, head_size, group_size, heads, topk, tile = dims
    rows = k_hbm.shape[0]
    hd = HEAD_DIMENSION
    chains = seq_size // group_size
    width = heads * hd
    me = lax.axis_index("seq")
    mine = lax.axis_index("head")
    plane = me // group_size
    place = me % group_size
    base = plane * group_size
    factor = math.log2(math.e) / math.sqrt(hd)
    others = [member(place, r, group_size) for r in range(group_size)]
    peers = [lax.rem(mine + h, head_size) for h in range(head_size)]
    has_next = plane < chains - 1
    has_prev = plane > 0
    ahead = me + group_size
    stagger = head_size == 2 and group_size > 1
    leads = mine == 0 if stagger else mine >= 0
    trails = mine == 1 if stagger else mine < 0

    w_copy = pltpu.make_async_copy(w_hbm, wbuf, w_sem)
    w_copy.start()

    barrier = pltpu.get_barrier_semaphore()
    for r in range(1, group_size):
        pl.semaphore_signal(barrier, inc=1, device_id={"seq": base + others[r]}, device_id_type=MESH)
    for h in range(1, head_size):
        pl.semaphore_signal(barrier, inc=1, device_id={"head": peers[h]}, device_id_type=MESH)

    @pl.when(has_next)
    def _():
        pl.semaphore_signal(barrier, inc=1, device_id={"seq": ahead}, device_id_type=MESH)

    @pl.when(has_prev)
    def _():
        pl.semaphore_signal(barrier, inc=1, device_id={"seq": me - group_size}, device_id_type=MESH)

    for g in range(group_size):
        v_own[g] = v_ref[:, g * hd:(g + 1) * hd].T
    near_count = jnp.where(has_next, 1, 0) + jnp.where(has_prev, 1, 0)
    pl.semaphore_wait(barrier, group_size + head_size - 2 + near_count)

    def k_piece(head):
        return k_hbm.at[:, pl.ds(pl.multiple_of(head * hd, hd), hd)]

    def v_piece(head):
        return v_own.at[head]

    def q_piece(head, i):
        return q_hbm.at[:, pl.ds(pl.multiple_of((head * heads + i) * hd, hd), hd)]

    def forward(a, k_src, v_src):
        return (
            pltpu.make_async_remote_copy(
                src_ref=k_src, dst_ref=kbuf.at[a], send_sem=k_fwd.at[a], recv_sem=k_recv.at[a],
                device_id={"seq": ahead}, device_id_type=MESH),
            pltpu.make_async_remote_copy(
                src_ref=v_src, dst_ref=vbuf.at[a], send_sem=v_fwd.at[a], recv_sem=v_recv.at[a],
                device_id={"seq": ahead}, device_id_type=MESH),
        )

    def relay(a):
        return forward(a, kbuf.at[a], vbuf.at[a])

    def to_member(r):
        t = others[r]
        kv = (
            pltpu.make_async_remote_copy(
                src_ref=k_piece(t), dst_ref=kbuf.at[me], send_sem=k_send.at[r], recv_sem=k_recv.at[me],
                device_id={"seq": base + t}, device_id_type=MESH),
            pltpu.make_async_remote_copy(
                src_ref=v_piece(t), dst_ref=vbuf.at[me], send_sem=v_send.at[r], recv_sem=v_recv.at[me],
                device_id={"seq": base + t}, device_id_type=MESH),
        )
        qs = [
            pltpu.make_async_remote_copy(
                src_ref=q_piece(t, i), dst_ref=qbuf[r].at[i], send_sem=q_send.at[r, i],
                recv_sem=q_recv.at[r, i], device_id={"seq": base + t}, device_id_type=MESH)
            for i in range(heads)
        ]
        return kv, qs

    def ids_copy(r):
        return pltpu.make_async_remote_copy(
            src_ref=ids_hbm, dst_ref=ids_in.at[r], send_sem=ids_send.at[r],
            recv_sem=ids_recv.at[r], device_id={"seq": base + others[r]}, device_id_type=MESH)

    def arrived(a):
        k_copy, v_copy = relay(a)
        k_copy.wait_recv()
        v_copy.wait_recv()

    def pass_on(a):
        @pl.when(has_next)
        def _():
            for copy in relay(a):
                copy.start()

    def open_gate(gate):
        if stagger:
            pl.semaphore_signal(gate, inc=1, device_id={"head": peers[1]}, device_id_type=MESH)

    ids_own = pltpu.make_async_copy(ids_hbm, ids_in.at[0], ids_send.at[0])
    ids_own.start()
    for r in range(1, group_size):
        ids_copy(r).start()
    sends = [None] + [to_member(r) for r in range(1, group_size)]
    own_first = forward(me, k_piece(place), v_piece(place))

    def send_own():
        @pl.when(has_next)
        def _():
            for copy in own_first:
                copy.start()

    def send_keys():
        for r in range(1, group_size):
            for copy in sends[r][0]:
                copy.start()

    def send_queries():
        for r in range(1, group_size):
            for copy in sends[r][1]:
                copy.start()

    send_own()

    @pl.when(leads)
    def _():
        send_keys()

    local = [
        pltpu.make_async_copy(k_piece(place), kbuf.at[me], k_send.at[0]),
        pltpu.make_async_copy(v_piece(place), vbuf.at[me], v_send.at[0]),
    ] + [pltpu.make_async_copy(q_piece(place, i), qbuf[0].at[i], q_send.at[0, i]) for i in range(heads)]
    for copy in local:
        copy.start()

    @pl.when(leads)
    def _():
        send_queries()

    for r in range(group_size):
        parts[r, seq_size] = jnp.zeros((hd, rows), jnp.bfloat16)
        stats[r, seq_size, 0:1, :] = jnp.full((1, rows), LOW, jnp.float32)
        stats[r, seq_size, 1:2, :] = jnp.zeros((1, rows), jnp.float32)
    for copy in local:
        copy.wait()

    causal = lax.broadcasted_iota(jnp.int32, (rows, rows), 0) <= lax.broadcasted_iota(
        jnp.int32, (rows, rows), 1)

    def diagonal(r):
        a = base + others[r]
        keep = jnp.concatenate([causal] * heads, axis=1)
        q = jnp.concatenate([qbuf[r][i] for i in range(heads)], axis=0)
        part, top, total = attend(kbuf[a], q, vbuf[a], factor, keep)
        for i in range(heads):
            span = slice(i * rows, (i + 1) * rows)
            own_parts[r, i] = part[:, span]
            own_stats[r, i, 0:1, :] = top[:, span]
            own_stats[r, i, 1:2, :] = total[:, span]

    def selected(members, a):
        q = jnp.concatenate([qbuf[r][table[r, a]] for r in members], axis=0)
        part, top, total = attend(kbuf[a], q, vbuf[a], factor, None)
        for n, r in enumerate(members):
            span = slice(n * rows, (n + 1) * rows)
            parts[r, a] = part[:, span]
            stats[r, a, 0:1, :] = top[:, span]
            stats[r, a, 1:2, :] = total[:, span]

    def block_at(t):
        level = t // group_size
        return base - (level + 1) * group_size + member(place, t % group_size, group_size)

    def inside(r, first):
        @pl.when(others[first] < others[r])
        def _():
            selected([r], base + others[first])

    def move(t):
        arrived(block_at(t))
        pass_on(block_at(t))

    diagonal(0)
    ids_own.wait()
    for r in range(1, group_size):
        ids_copy(r).wait_recv()
    ids_local = pltpu.make_async_copy(ids_in, ids, ids_sem)
    ids_local.start()
    ids_local.wait()

    picks = [(i, j) for i in range(heads) for j in range(topk)]

    def pick(r, i, j):
        return ids[r, j, 0, place * heads + i]

    def note(a, carry):
        for r in range(group_size):
            head = 0
            for i, j in picks:
                head = jnp.where(pick(r, i, j) == a, i, head)
            table[r, a] = head
        return carry

    @pl.when(trails)
    def _():
        if stagger:
            pl.semaphore_wait(kv_gate, 1)
        send_keys()

    lax.fori_loop(0, base + group_size, note, 0)

    for r in range(1, group_size):
        arrived(base + others[r])

        @pl.when(leads)
        def _():
            pass_on(base + others[r])

    @pl.when(leads)
    def _():
        open_gate(kv_gate)

    for r in range(1, group_size):
        inside(0, r)

    @pl.when(trails)
    def _():
        if stagger:
            pl.semaphore_wait(q_gate, 1)
        send_queries()

    @pl.when(leads & has_prev)
    def _():
        for t in range(group_size):
            move(t)

    def begin_chain():
        if stagger:
            pl.semaphore_wait(chain_gate, 1)
        for r in range(1, group_size):
            pass_on(base + others[r])

    levels_two = plane > 1

    @pl.when(leads & has_next)
    def _():
        open_gate(chain_gate)

    @pl.when(trails & has_next)
    def _():
        begin_chain()

    for r in range(1, group_size):
        for copy in sends[r][1]:
            copy.wait_recv()
        if r == 1:
            @pl.when(leads)
            def _():
                open_gate(q_gate)
        diagonal(r)

    for r in range(1, group_size):
        for first in range(group_size):
            if first != r:
                inside(r, first)

    def far(t, carry):
        selected(range(group_size), block_at(t))
        return carry

    def far_move(t, carry):
        move(t)
        return far(t, carry)

    def near(t, carry):
        @pl.when(levels_two)
        def _():
            move(t + group_size)
        return far(t, carry)

    @pl.when(leads & has_prev)
    def _():
        lax.fori_loop(0, group_size, near, 0)

    @pl.when(leads & levels_two)
    def _():
        lax.fori_loop(group_size, 2 * group_size, far, 0)
        lax.fori_loop(2 * group_size, plane * group_size, far_move, 0)

    @pl.when(trails)
    def _():
        lax.fori_loop(0, plane * group_size, far_move, 0)

    def att_copy(r, i):
        return pltpu.make_async_remote_copy(
            src_ref=att_out.at[r, i], dst_ref=att_in.at[place, i], send_sem=att_send.at[r, i],
            recv_sem=att_recv.at[r, i], device_id={"seq": base + others[r]}, device_id_type=MESH)

    direct = [r for r in range(1, group_size) if not r & (r - 1)]
    through = [r for r in range(1, group_size) if r & (r - 1)] + [0]
    steps = [(r, i) for i in range(heads) for r in direct] + [(r, i) for r in through for i in range(heads)]
    for r, i in steps:
        block = base + others[r]
        tops = [own_stats[r, i, 0:1, :]]
        totals = [own_stats[r, i, 1:2, :]]
        slots = [jnp.where(pick(r, i, j) < block, pick(r, i, j), seq_size) for j in range(topk)]
        for slot in slots:
            tops.append(stats[r, slot, 0:1, :])
            totals.append(stats[r, slot, 1:2, :])
        top = functools.reduce(jnp.maximum, tops)
        weights = [jnp.exp2((one - top) * factor) for one in tops]
        inverse = 1.0 / sum(w * t for w, t in zip(weights, totals))
        weights = [w * inverse for w in weights]
        accum = weights[0] * own_parts[r, i].astype(jnp.float32)
        for slot, weight in zip(slots, weights[1:]):
            accum = accum + weight * parts[r, slot].astype(jnp.float32)
        attended = accum.astype(jnp.bfloat16).T
        if r:
            att_out[r, i] = attended
        else:
            att_in[place, i] = attended
        if r:
            att_copy(r, i).start()

    features = w_hbm.shape[1] // head_size
    tiles = features // tile

    def product(r, start):
        row = pl.multiple_of(others[r] * width, width)
        rows_in = jnp.concatenate([att_in[others[r], i] for i in range(heads)], axis=1)
        return jnp.dot(
            rows_in, wbuf[pl.ds(row, width), pl.ds(start, tile)],
            preferred_element_type=jnp.float32)

    w_copy.wait()

    def share(early, members):
        for r in members:
            if r:
                for i in range(heads):
                    att_copy(r, i).wait_recv()

        def one(n, carry):
            terms = [product(r, pl.multiple_of(n * tile, tile)) for r in members]
            acc[n] = sum(terms) if early else acc[n] + sum(terms)
            return carry

        if members:
            lax.fori_loop(0, head_size * tiles, one, 0)

    share(True, list(range(min(1, group_size - 1))))
    for r in range(1, group_size - 1):
        share(False, [r])
    if group_size > 1:
        for i in range(heads):
            att_copy(group_size - 1, i).wait_recv()

    def project(peer, n):
        result = product(group_size - 1, pl.multiple_of(peer * features + n * tile, tile))
        if group_size > 1:
            result = result + acc[peer * tiles + n]
        return result.astype(jnp.bfloat16)

    def piece_copy(h, n):
        return pltpu.make_async_remote_copy(
            src_ref=piece_out.at[h - 1, n], dst_ref=piece_in.at[h - 1, n],
            send_sem=piece_send.at[h - 1, n], recv_sem=piece_recv.at[h - 1, n],
            device_id={"head": peers[h]}, device_id_type=MESH)

    for h in range(1, head_size):
        def give(n, carry):
            piece_out[h - 1, n] = project(peers[h], n)
            piece_copy(h, n).start()
            return carry
        lax.fori_loop(0, tiles, give, 0)

    def finish(n, carry):
        total = project(mine, n).astype(jnp.float32)
        for h in range(1, head_size):
            piece_copy(h, n).wait_recv()
            total = total + piece_in[h - 1, n].astype(jnp.float32)
        out_ref[n] = total.astype(jnp.bfloat16)
        return carry

    lax.fori_loop(0, tiles, finish, 0)

    for h in range(1, head_size):
        for n in range(tiles):
            piece_copy(h, n).wait_send()
    for r in range(1, group_size):
        ids_copy(r).wait_send()
        for i in range(heads):
            att_copy(r, i).wait_send()
        for copy in sends[r][0]:
            copy.wait_send()
        for copy in sends[r][1]:
            copy.wait_send()

    @pl.when(has_next)
    def _():
        def gone(a, carry):
            for copy in relay(a):
                copy.wait_send()
            return carry
        lax.fori_loop(0, base + group_size, gone, 0)


def flip(x_ref, out_ref):
    out_ref[...] = x_ref[0].T


def local(seq_size, head_size, queries, keys, values, block_ids, out_weight):
    rows = queries.shape[0]
    hd = HEAD_DIMENSION
    kv_heads = keys.shape[1] // hd
    heads = queries.shape[1] // hd // kv_heads
    topk = block_ids.shape[2]
    model = out_weight.shape[1]
    features = model // head_size
    tile = min(1024, features)
    ids = jnp.transpose(block_ids, (2, 0, 1))
    bf16, f32 = jnp.bfloat16, jnp.float32
    tiles = features // tile
    dma = pltpu.SemaphoreType.DMA
    g = kv_heads
    hbm = pl.BlockSpec(memory_space=pl.ANY)
    more = max(head_size - 1, 1)
    result = pl.pallas_call(
        functools.partial(kernel, (seq_size, head_size, g, heads, topk, tile)),
        out_shape=jax.ShapeDtypeStruct((tiles, rows, tile), bf16),
        in_specs=[hbm, hbm, hbm, pl.BlockSpec(memory_space=pltpu.VMEM), hbm],
        out_specs=pl.BlockSpec(memory_space=pltpu.VMEM),
        scratch_shapes=[
            pltpu.VMEM((seq_size, rows, hd), bf16),
            pltpu.VMEM((seq_size, hd, rows), bf16),
            pltpu.VMEM((g, seq_size + 1, hd, rows), bf16),
            pltpu.VMEM((g, seq_size + 1, 8, rows), f32),
            pltpu.VMEM((g, heads, hd, rows), bf16),
            pltpu.VMEM((g, heads, 8, rows), f32),
            pltpu.VMEM(out_weight.shape, bf16),
            pltpu.VMEM((g, heads, rows, hd), bf16),
            pltpu.VMEM((g, heads, rows, hd), bf16),
            pltpu.VMEM((more, tiles, rows, tile), bf16),
            pltpu.VMEM((more, tiles, rows, tile), bf16),
            pltpu.VMEM((g, hd, rows), bf16),
            pltpu.VMEM((g, *ids.shape), jnp.int32),
            pltpu.SMEM((g, *ids.shape), jnp.int32),
            pltpu.SMEM((g, seq_size), jnp.int32),
            pltpu.VMEM((head_size * tiles, rows, tile), f32),
            dma((seq_size,)), dma((seq_size,)), dma((seq_size,)), dma((seq_size,)),
            dma((g,)), dma((g,)), dma((g, heads)), dma((g, heads)),
            dma((g, heads)), dma((g, heads)), dma((more, tiles)), dma((more, tiles)), dma,
            dma((g,)), dma((g,)), dma,
        ] + [pltpu.SemaphoreType.REGULAR] * 3 + [pltpu.VMEM((heads, rows, hd), bf16)] * g,
        compiler_params=pltpu.CompilerParams(
            collective_id=0, has_side_effects=True, vmem_limit_bytes=60 << 20),
    )(ids, queries, keys, values, out_weight)
    return pl.pallas_call(
        flip,
        grid=(tiles,),
        out_shape=jax.ShapeDtypeStruct((features, rows), bf16),
        in_specs=[pl.BlockSpec((1, rows, tile), lambda n: (n, 0, 0))],
        out_specs=pl.BlockSpec((tile, rows), lambda n: (n, 0)),
    )(result)


def solution(mesh):
    return jax.shard_map(
        functools.partial(local, mesh.shape["seq"], mesh.shape["head"]),
        mesh=mesh,
        in_specs=(
            P("seq", "head"),
            P("seq", "head"),
            P("seq", "head"),
            P("seq", "head", None),
            P("head", None),
        ),
        out_specs=P("head", "seq"),
        check_vma=False,
    )
```

```python
import functools
import math

import jax
import jax.numpy as jnp
from jax import lax
from jax.experimental import pallas as pl
from jax.experimental.pallas import tpu as pltpu
from jax.sharding import PartitionSpec as P

HEAD_DIMENSION = 128
MESH = pl.DeviceIdType.MESH
LOW = -1e30


def member(position, step, size):
    if size & (size - 1):
        return lax.rem(step - position + size, size)
    other, bit = 0, 1
    while bit < size:
        digit = (position // bit) % 2
        other = other + bit * ((digit + (step // bit) % 2) % 2)
        bit *= 2
    return other


def attend(k, q, v_t, factor, keep):
    scores = lax.dot_general(k, q, (((1,), (1,)), ((), ())), preferred_element_type=jnp.float32)
    if keep is not None:
        scores = jnp.where(keep, scores, LOW)
    top = jnp.max(scores, axis=0, keepdims=True)
    prob = jnp.exp2((scores - top) * factor)
    total = jnp.sum(prob, axis=0, keepdims=True)
    part = jnp.dot(v_t, prob.astype(jnp.bfloat16), preferred_element_type=jnp.float32)
    return part.astype(jnp.bfloat16), top, total


def kernel(
    dims,
    ids_hbm, q_hbm, k_hbm, v_ref, w_hbm,
    out_ref,
    kbuf, vbuf, parts, stats, own_parts, own_stats, wbuf,
    att_out, att_in, piece_out, piece_in, v_own, ids_in, ids, table, acc,
    k_recv, v_recv, k_fwd, v_fwd, k_send, v_send, q_send, q_recv,
    att_send, att_recv, piece_send, piece_recv, w_sem,
    ids_send, ids_recv, ids_sem, kv_gate, q_gate, chain_gate, out_buf, out_sem, *qbuf,
):
    seq_size, head_size, group_size, heads, topk, tile = dims
    rows = k_hbm.shape[0]
    hd = HEAD_DIMENSION
    chains = seq_size // group_size
    width = heads * hd
    me = lax.axis_index("seq")
    mine = lax.axis_index("head")
    plane = me // group_size
    place = me % group_size
    base = plane * group_size
    factor = math.log2(math.e) / math.sqrt(hd)
    others = [member(place, r, group_size) for r in range(group_size)]
    peers = [lax.rem(mine + h, head_size) for h in range(head_size)]
    has_next = plane < chains - 1
    has_prev = plane > 0
    ahead = me + group_size
    stagger = head_size == 2 and group_size > 1
    leads = mine == 0 if stagger else mine >= 0
    trails = mine == 1 if stagger else mine < 0

    w_copy = pltpu.make_async_copy(w_hbm, wbuf, w_sem)
    w_copy.start()

    barrier = pltpu.get_barrier_semaphore()
    for r in range(1, group_size):
        pl.semaphore_signal(barrier, inc=1, device_id={"seq": base + others[r]}, device_id_type=MESH)
    for h in range(1, head_size):
        pl.semaphore_signal(barrier, inc=1, device_id={"head": peers[h]}, device_id_type=MESH)

    @pl.when(has_next)
    def _():
        pl.semaphore_signal(barrier, inc=1, device_id={"seq": ahead}, device_id_type=MESH)

    @pl.when(has_prev)
    def _():
        pl.semaphore_signal(barrier, inc=1, device_id={"seq": me - group_size}, device_id_type=MESH)

    for g in range(group_size):
        v_own[g] = v_ref[:, g * hd:(g + 1) * hd].T
    near_count = jnp.where(has_next, 1, 0) + jnp.where(has_prev, 1, 0)
    pl.semaphore_wait(barrier, group_size + head_size - 2 + near_count)

    def k_piece(head):
        return k_hbm.at[:, pl.ds(pl.multiple_of(head * hd, hd), hd)]

    def v_piece(head):
        return v_own.at[head]

    def q_piece(head, i):
        return q_hbm.at[:, pl.ds(pl.multiple_of((head * heads + i) * hd, hd), hd)]

    def forward(a, k_src, v_src):
        return (
            pltpu.make_async_remote_copy(
                src_ref=k_src, dst_ref=kbuf.at[a], send_sem=k_fwd.at[a], recv_sem=k_recv.at[a],
                device_id={"seq": ahead}, device_id_type=MESH),
            pltpu.make_async_remote_copy(
                src_ref=v_src, dst_ref=vbuf.at[a], send_sem=v_fwd.at[a], recv_sem=v_recv.at[a],
                device_id={"seq": ahead}, device_id_type=MESH),
        )

    def relay(a):
        return forward(a, kbuf.at[a], vbuf.at[a])

    def to_member(r):
        t = others[r]
        kv = (
            pltpu.make_async_remote_copy(
                src_ref=k_piece(t), dst_ref=kbuf.at[me], send_sem=k_send.at[r], recv_sem=k_recv.at[me],
                device_id={"seq": base + t}, device_id_type=MESH),
            pltpu.make_async_remote_copy(
                src_ref=v_piece(t), dst_ref=vbuf.at[me], send_sem=v_send.at[r], recv_sem=v_recv.at[me],
                device_id={"seq": base + t}, device_id_type=MESH),
        )
        qs = [
            pltpu.make_async_remote_copy(
                src_ref=q_piece(t, i), dst_ref=qbuf[r].at[i], send_sem=q_send.at[r, i],
                recv_sem=q_recv.at[r, i], device_id={"seq": base + t}, device_id_type=MESH)
            for i in range(heads)
        ]
        return kv, qs

    def ids_copy(r):
        return pltpu.make_async_remote_copy(
            src_ref=ids_hbm, dst_ref=ids_in.at[r], send_sem=ids_send.at[r],
            recv_sem=ids_recv.at[r], device_id={"seq": base + others[r]}, device_id_type=MESH)

    def arrived(a):
        k_copy, v_copy = relay(a)
        k_copy.wait_recv()
        v_copy.wait_recv()

    def pass_on(a):
        @pl.when(has_next)
        def _():
            for copy in relay(a):
                copy.start()

    def open_gate(gate):
        if stagger:
            pl.semaphore_signal(gate, inc=1, device_id={"head": peers[1]}, device_id_type=MESH)

    ids_own = pltpu.make_async_copy(ids_hbm, ids_in.at[0], ids_send.at[0])
    ids_own.start()
    for r in range(1, group_size):
        ids_copy(r).start()
    sends = [None] + [to_member(r) for r in range(1, group_size)]
    own_first = forward(me, k_piece(place), v_piece(place))

    def send_own():
        @pl.when(has_next)
        def _():
            for copy in own_first:
                copy.start()

    def send_keys():
        for r in range(1, group_size):
            for copy in sends[r][0]:
                copy.start()

    def send_queries():
        for r in range(1, group_size):
            for copy in sends[r][1]:
                copy.start()

    send_own()

    @pl.when(leads)
    def _():
        send_keys()

    local = [
        pltpu.make_async_copy(k_piece(place), kbuf.at[me], k_send.at[0]),
        pltpu.make_async_copy(v_piece(place), vbuf.at[me], v_send.at[0]),
    ] + [pltpu.make_async_copy(q_piece(place, i), qbuf[0].at[i], q_send.at[0, i]) for i in range(heads)]
    for copy in local:
        copy.start()

    @pl.when(leads)
    def _():
        send_queries()

    for r in range(group_size):
        parts[r, seq_size] = jnp.zeros((hd, rows), jnp.bfloat16)
        stats[r, seq_size, 0:1, :] = jnp.full((1, rows), LOW, jnp.float32)
        stats[r, seq_size, 1:2, :] = jnp.zeros((1, rows), jnp.float32)
    for copy in local:
        copy.wait()

    causal = lax.broadcasted_iota(jnp.int32, (rows, rows), 0) <= lax.broadcasted_iota(
        jnp.int32, (rows, rows), 1)

    def diagonal(r):
        a = base + others[r]
        keep = jnp.concatenate([causal] * heads, axis=1)
        q = jnp.concatenate([qbuf[r][i] for i in range(heads)], axis=0)
        part, top, total = attend(kbuf[a], q, vbuf[a], factor, keep)
        for i in range(heads):
            span = slice(i * rows, (i + 1) * rows)
            own_parts[r, i] = part[:, span]
            own_stats[r, i, 0:1, :] = top[:, span]
            own_stats[r, i, 1:2, :] = total[:, span]

    def selected(members, a):
        q = jnp.concatenate([qbuf[r][table[r, a]] for r in members], axis=0)
        part, top, total = attend(kbuf[a], q, vbuf[a], factor, None)
        for n, r in enumerate(members):
            span = slice(n * rows, (n + 1) * rows)
            parts[r, a] = part[:, span]
            stats[r, a, 0:1, :] = top[:, span]
            stats[r, a, 1:2, :] = total[:, span]

    def block_at(t):
        level = t // group_size
        return base - (level + 1) * group_size + member(place, t % group_size, group_size)

    def inside(r, first):
        @pl.when(others[first] < others[r])
        def _():
            selected([r], base + others[first])

    def move(t):
        arrived(block_at(t))
        pass_on(block_at(t))

    diagonal(0)
    ids_own.wait()
    for r in range(1, group_size):
        ids_copy(r).wait_recv()
    ids_local = pltpu.make_async_copy(ids_in, ids, ids_sem)
    ids_local.start()
    ids_local.wait()

    picks = [(i, j) for i in range(heads) for j in range(topk)]

    def pick(r, i, j):
        return ids[r, j, 0, place * heads + i]

    def note(a, carry):
        for r in range(group_size):
            head = 0
            for i, j in picks:
                head = jnp.where(pick(r, i, j) == a, i, head)
            table[r, a] = head
        return carry

    @pl.when(trails)
    def _():
        if stagger:
            pl.semaphore_wait(kv_gate, 1)
        send_keys()

    lax.fori_loop(0, base + group_size, note, 0)

    for r in range(1, group_size):
        arrived(base + others[r])

        @pl.when(leads)
        def _():
            pass_on(base + others[r])

    @pl.when(leads)
    def _():
        open_gate(kv_gate)

    for r in range(1, group_size):
        inside(0, r)

    @pl.when(trails)
    def _():
        if stagger:
            pl.semaphore_wait(q_gate, 1)
        send_queries()

    @pl.when(leads & has_prev)
    def _():
        for t in range(group_size):
            move(t)

    def begin_chain():
        if stagger:
            pl.semaphore_wait(chain_gate, 1)
        for r in range(1, group_size):
            pass_on(base + others[r])

    levels_two = plane > 1

    @pl.when(leads & has_next)
    def _():
        open_gate(chain_gate)

    @pl.when(trails & has_next)
    def _():
        begin_chain()

    for r in range(1, group_size):
        for copy in sends[r][1]:
            copy.wait_recv()
        if r == 1:
            @pl.when(leads)
            def _():
                open_gate(q_gate)
        diagonal(r)

    for r in range(1, group_size):
        for first in range(group_size):
            if first != r:
                inside(r, first)

    def far(t, carry):
        selected(range(group_size), block_at(t))
        return carry

    def far_move(t, carry):
        move(t)
        return far(t, carry)

    def near(t, carry):
        @pl.when(levels_two)
        def _():
            move(t + group_size)
        return far(t, carry)

    @pl.when(leads & has_prev)
    def _():
        lax.fori_loop(0, group_size, near, 0)

    @pl.when(leads & levels_two)
    def _():
        lax.fori_loop(group_size, 2 * group_size, far, 0)
        lax.fori_loop(2 * group_size, plane * group_size, far_move, 0)

    @pl.when(trails)
    def _():
        lax.fori_loop(0, plane * group_size - 1, far_move, 0)

    def att_copy(r, i):
        return pltpu.make_async_remote_copy(
            src_ref=att_out.at[r, i], dst_ref=att_in.at[place, i], send_sem=att_send.at[r, i],
            recv_sem=att_recv.at[r, i], device_id={"seq": base + others[r]}, device_id_type=MESH)

    near_ones = [r for r in range(1, group_size) if not r & (r - 1)]
    far_ones = [r for r in range(1, group_size) if r & (r - 1)] + [0]

    def give_back(r, i):
        block = base + others[r]
        tops = [own_stats[r, i, 0:1, :]]
        totals = [own_stats[r, i, 1:2, :]]
        slots = [jnp.where(pick(r, i, j) < block, pick(r, i, j), seq_size) for j in range(topk)]
        for slot in slots:
            tops.append(stats[r, slot, 0:1, :])
            totals.append(stats[r, slot, 1:2, :])
        top = functools.reduce(jnp.maximum, tops)
        weights = [jnp.exp2((one - top) * factor) for one in tops]
        inverse = 1.0 / sum(w * t for w, t in zip(weights, totals))
        weights = [w * inverse for w in weights]
        accum = weights[0] * own_parts[r, i].astype(jnp.float32)
        for slot, weight in zip(slots, weights[1:]):
            accum = accum + weight * parts[r, slot].astype(jnp.float32)
        attended = accum.astype(jnp.bfloat16).T
        if r:
            att_out[r, i] = attended
        else:
            att_in[place, i] = attended
        if r:
            att_copy(r, i).start()

    final = plane * group_size - 1

    @pl.when(trails & has_prev)
    def _():
        move(final)

    for members in (near_ones, far_ones):
        if members:
            @pl.when(trails & has_prev)
            def _():
                selected(members, block_at(final))

            for i in range(heads):
                for r in members:
                    give_back(r, i)

    features = w_hbm.shape[1] // head_size
    tiles = features // tile

    def product(r, start, span):
        row = pl.multiple_of(others[r] * width, width)
        rows_in = jnp.concatenate([att_in[others[r], i] for i in range(heads)], axis=1)
        return jnp.dot(
            rows_in, wbuf[pl.ds(row, width), pl.ds(start, span)],
            preferred_element_type=jnp.float32)

    w_copy.wait()

    def share(early, members):
        for r in members:
            if r:
                for i in range(heads):
                    att_copy(r, i).wait_recv()

        def one(n, carry):
            terms = [product(r, pl.multiple_of(n * tile, tile), tile) for r in members]
            acc[n] = sum(terms) if early else acc[n] + sum(terms)
            return carry

        if members:
            lax.fori_loop(0, head_size * tiles, one, 0)

    share(True, list(range(min(1, group_size - 1))))
    for r in range(1, group_size - 1):
        share(False, [r])
    if group_size > 1:
        for i in range(heads):
            att_copy(group_size - 1, i).wait_recv()

    piece = piece_out.shape[3]
    split = tile // piece

    def project(peer, n, u):
        result = product(
            group_size - 1, pl.multiple_of(peer * features + n * tile + u * piece, piece), piece)
        if group_size > 1:
            result = result + acc[peer * tiles + n][:, u * piece:(u + 1) * piece]
        return result.astype(jnp.bfloat16)

    def piece_copy(h, n):
        return pltpu.make_async_remote_copy(
            src_ref=piece_out.at[h - 1, n], dst_ref=piece_in.at[h - 1, n],
            send_sem=piece_send.at[h - 1, n], recv_sem=piece_recv.at[h - 1, n],
            device_id={"head": peers[h]}, device_id_type=MESH)

    for h in range(1, head_size):
        def give(n, carry):
            for u in range(split):
                piece_out[h - 1, n * split + u] = project(peers[h], n, u)
                piece_copy(h, n * split + u).start()
            return carry
        lax.fori_loop(0, tiles, give, 0)

    def out_copy(n):
        return pltpu.make_async_copy(out_buf.at[n], out_ref.at[n], out_sem.at[n])

    def finish(n, carry):
        for u in range(split):
            total = project(mine, n, u).astype(jnp.float32)
            for h in range(1, head_size):
                piece_copy(h, n * split + u).wait_recv()
                total = total + piece_in[h - 1, n * split + u].astype(jnp.float32)
            out_buf[n * split + u] = total.astype(jnp.bfloat16)
            out_copy(n * split + u).start()
        return carry

    lax.fori_loop(0, tiles, finish, 0)
    for n in range(tiles * split):
        out_copy(n).wait()

    for h in range(1, head_size):
        for n in range(tiles * split):
            piece_copy(h, n).wait_send()
    for r in range(1, group_size):
        ids_copy(r).wait_send()
        for i in range(heads):
            att_copy(r, i).wait_send()
        for copy in sends[r][0]:
            copy.wait_send()
        for copy in sends[r][1]:
            copy.wait_send()

    @pl.when(has_next)
    def _():
        def gone(a, carry):
            for copy in relay(a):
                copy.wait_send()
            return carry
        lax.fori_loop(0, base + group_size, gone, 0)


def flip(x_hbm, out_hbm, x_buf, out_buf, x_sem, out_sem):
    parts, rows, span = x_buf.shape
    each = x_hbm.shape[2] // span
    reads, writes = [], []
    for n in range(parts):
        reads.append(pltpu.make_async_copy(
            x_hbm.at[n // each, :, pl.ds((n % each) * span, span)], x_buf.at[n], x_sem.at[n]))
        writes.append(pltpu.make_async_copy(
            out_buf.at[n], out_hbm.at[pl.ds(n * span, span), :], out_sem.at[n]))
    for copy in reads:
        copy.start()
    for n in range(parts):
        reads[n].wait()
        out_buf[n] = x_buf[n].T
        writes[n].start()
    for copy in writes:
        copy.wait()


def local(seq_size, head_size, queries, keys, values, block_ids, out_weight):
    rows = queries.shape[0]
    hd = HEAD_DIMENSION
    kv_heads = keys.shape[1] // hd
    heads = queries.shape[1] // hd // kv_heads
    topk = block_ids.shape[2]
    model = out_weight.shape[1]
    features = model // head_size
    tile = min(1024, features)
    piece = min(512, tile)
    pieces = features // piece
    ids = jnp.transpose(block_ids, (2, 0, 1))
    bf16, f32 = jnp.bfloat16, jnp.float32
    tiles = features // tile
    dma = pltpu.SemaphoreType.DMA
    g = kv_heads
    hbm = pl.BlockSpec(memory_space=pl.ANY)
    more = max(head_size - 1, 1)
    result = pl.pallas_call(
        functools.partial(kernel, (seq_size, head_size, g, heads, topk, tile)),
        out_shape=jax.ShapeDtypeStruct((pieces, rows, piece), bf16),
        in_specs=[hbm, hbm, hbm, pl.BlockSpec(memory_space=pltpu.VMEM), hbm],
        out_specs=hbm,
        scratch_shapes=[
            pltpu.VMEM((seq_size, rows, hd), bf16),
            pltpu.VMEM((seq_size, hd, rows), bf16),
            pltpu.VMEM((g, seq_size + 1, hd, rows), bf16),
            pltpu.VMEM((g, seq_size + 1, 8, rows), f32),
            pltpu.VMEM((g, heads, hd, rows), bf16),
            pltpu.VMEM((g, heads, 8, rows), f32),
            pltpu.VMEM(out_weight.shape, bf16),
            pltpu.VMEM((g, heads, rows, hd), bf16),
            pltpu.VMEM((g, heads, rows, hd), bf16),
            pltpu.VMEM((more, pieces, rows, piece), bf16),
            pltpu.VMEM((more, pieces, rows, piece), bf16),
            pltpu.VMEM((g, hd, rows), bf16),
            pltpu.VMEM((g, *ids.shape), jnp.int32),
            pltpu.SMEM((g, *ids.shape), jnp.int32),
            pltpu.SMEM((g, seq_size), jnp.int32),
            pltpu.VMEM((head_size * tiles, rows, tile), f32),
            dma((seq_size,)), dma((seq_size,)), dma((seq_size,)), dma((seq_size,)),
            dma((g,)), dma((g,)), dma((g, heads)), dma((g, heads)),
            dma((g, heads)), dma((g, heads)), dma((more, pieces)), dma((more, pieces)), dma,
            dma((g,)), dma((g,)), dma,
        ] + [pltpu.SemaphoreType.REGULAR] * 3 + [
            pltpu.VMEM((pieces, rows, piece), bf16), dma((pieces,)),
        ] + [pltpu.VMEM((heads, rows, hd), bf16)] * g,
        compiler_params=pltpu.CompilerParams(
            collective_id=0, has_side_effects=True, vmem_limit_bytes=60 << 20),
    )(ids, queries, keys, values, out_weight)
    span = min(256, piece)
    count = features // span
    return pl.pallas_call(
        flip,
        out_shape=jax.ShapeDtypeStruct((features, rows), bf16),
        in_specs=[hbm],
        out_specs=hbm,
        scratch_shapes=[
            pltpu.VMEM((count, rows, span), bf16),
            pltpu.VMEM((count, span, rows), bf16),
            dma((count,)), dma((count,)),
        ],
    )(result)


def solution(mesh):
    return jax.shard_map(
        functools.partial(local, mesh.shape["seq"], mesh.shape["head"]),
        mesh=mesh,
        in_specs=(
            P("seq", "head"),
            P("seq", "head"),
            P("seq", "head"),
            P("seq", "head", None),
            P("head", None),
        ),
        out_specs=P("head", "seq"),
        check_vma=False,
    )
```

```python
import functools
import math

import jax
import jax.numpy as jnp
from jax import lax
from jax.experimental import pallas as pl
from jax.experimental.pallas import tpu as pltpu
from jax.sharding import PartitionSpec as P

HEAD_DIMENSION = 128
MESH = pl.DeviceIdType.MESH
LOW = -1e30


def member(position, step, size):
    if size & (size - 1):
        return lax.rem(step - position + size, size)
    other, bit = 0, 1
    while bit < size:
        digit = (position // bit) % 2
        other = other + bit * ((digit + (step // bit) % 2) % 2)
        bit *= 2
    return other


def attend(k, q, v_t, factor, keep):
    scores = lax.dot_general(k, q, (((1,), (1,)), ((), ())), preferred_element_type=jnp.float32)
    if keep is not None:
        scores = jnp.where(keep, scores, LOW)
    top = jnp.max(scores, axis=0, keepdims=True)
    prob = jnp.exp2((scores - top) * factor)
    total = jnp.sum(prob, axis=0, keepdims=True)
    part = jnp.dot(v_t, prob.astype(jnp.bfloat16), preferred_element_type=jnp.float32)
    return part.astype(jnp.bfloat16), top, total


def kernel(
    dims,
    ids_hbm, q_hbm, k_hbm, v_ref, w_hbm,
    out_ref,
    kbuf, vbuf, parts, stats, own_parts, own_stats, wbuf,
    att_out, att_in, piece_out, piece_in, v_own, ids_in, ids, table, acc,
    k_recv, v_recv, k_fwd, v_fwd, k_send, v_send, q_send, q_recv,
    att_send, att_recv, piece_send, piece_recv, w_sem,
    ids_send, ids_recv, ids_sem, kv_gate, q_gate, chain_gate, out_buf, out_sem, *qbuf,
):
    seq_size, head_size, group_size, heads, topk, tile = dims
    rows = k_hbm.shape[0]
    hd = HEAD_DIMENSION
    chains = seq_size // group_size
    width = heads * hd
    me = lax.axis_index("seq")
    mine = lax.axis_index("head")
    plane = me // group_size
    place = me % group_size
    base = plane * group_size
    factor = math.log2(math.e) / math.sqrt(hd)
    others = [member(place, r, group_size) for r in range(group_size)]
    peers = [lax.rem(mine + h, head_size) for h in range(head_size)]
    has_next = plane < chains - 1
    has_prev = plane > 0
    ahead = me + group_size
    stagger = head_size == 2 and group_size > 1
    leads = mine == 0 if stagger else mine >= 0
    trails = mine == 1 if stagger else mine < 0

    w_copy = pltpu.make_async_copy(w_hbm, wbuf, w_sem)
    w_copy.start()

    barrier = pltpu.get_barrier_semaphore()
    for r in range(1, group_size):
        pl.semaphore_signal(barrier, inc=1, device_id={"seq": base + others[r]}, device_id_type=MESH)
    for h in range(1, head_size):
        pl.semaphore_signal(barrier, inc=1, device_id={"head": peers[h]}, device_id_type=MESH)

    @pl.when(has_next)
    def _():
        pl.semaphore_signal(barrier, inc=1, device_id={"seq": ahead}, device_id_type=MESH)

    @pl.when(has_prev)
    def _():
        pl.semaphore_signal(barrier, inc=1, device_id={"seq": me - group_size}, device_id_type=MESH)

    for g in range(group_size):
        v_own[g] = v_ref[:, g * hd:(g + 1) * hd].T
    near_count = jnp.where(has_next, 1, 0) + jnp.where(has_prev, 1, 0)
    pl.semaphore_wait(barrier, group_size + head_size - 2 + near_count)

    def k_piece(head):
        return k_hbm.at[:, pl.ds(pl.multiple_of(head * hd, hd), hd)]

    def v_piece(head):
        return v_own.at[head]

    def q_piece(head, i):
        return q_hbm.at[:, pl.ds(pl.multiple_of((head * heads + i) * hd, hd), hd)]

    def forward(a, k_src, v_src):
        return (
            pltpu.make_async_remote_copy(
                src_ref=k_src, dst_ref=kbuf.at[a], send_sem=k_fwd.at[a], recv_sem=k_recv.at[a],
                device_id={"seq": ahead}, device_id_type=MESH),
            pltpu.make_async_remote_copy(
                src_ref=v_src, dst_ref=vbuf.at[a], send_sem=v_fwd.at[a], recv_sem=v_recv.at[a],
                device_id={"seq": ahead}, device_id_type=MESH),
        )

    def relay(a):
        return forward(a, kbuf.at[a], vbuf.at[a])

    def to_member(r):
        t = others[r]
        kv = (
            pltpu.make_async_remote_copy(
                src_ref=k_piece(t), dst_ref=kbuf.at[me], send_sem=k_send.at[r], recv_sem=k_recv.at[me],
                device_id={"seq": base + t}, device_id_type=MESH),
            pltpu.make_async_remote_copy(
                src_ref=v_piece(t), dst_ref=vbuf.at[me], send_sem=v_send.at[r], recv_sem=v_recv.at[me],
                device_id={"seq": base + t}, device_id_type=MESH),
        )
        qs = [
            pltpu.make_async_remote_copy(
                src_ref=q_piece(t, i), dst_ref=qbuf[r].at[i], send_sem=q_send.at[r, i],
                recv_sem=q_recv.at[r, i], device_id={"seq": base + t}, device_id_type=MESH)
            for i in range(heads)
        ]
        return kv, qs

    def ids_copy(r):
        return pltpu.make_async_remote_copy(
            src_ref=ids_hbm, dst_ref=ids_in.at[r], send_sem=ids_send.at[r],
            recv_sem=ids_recv.at[r], device_id={"seq": base + others[r]}, device_id_type=MESH)

    def pass_on(a):
        @pl.when(has_next)
        def _():
            for copy in relay(a):
                copy.start()

    def open_gate(gate):
        if stagger:
            pl.semaphore_signal(gate, inc=1, device_id={"head": peers[1]}, device_id_type=MESH)

    ids_own = pltpu.make_async_copy(ids_hbm, ids_in.at[0], ids_send.at[0])
    ids_own.start()
    for r in range(1, group_size):
        ids_copy(r).start()
    sends = [None] + [to_member(r) for r in range(1, group_size)]
    own_first = forward(me, k_piece(place), v_piece(place))

    def send_own():
        @pl.when(has_next)
        def _():
            for copy in own_first:
                copy.start()

    def send_keys():
        for r in range(1, group_size):
            for copy in sends[r][0]:
                copy.start()

    def send_queries():
        for r in range(1, group_size):
            for copy in sends[r][1]:
                copy.start()

    send_own()

    @pl.when(leads)
    def _():
        send_keys()

    local = [
        pltpu.make_async_copy(k_piece(place), kbuf.at[me], k_send.at[0]),
        pltpu.make_async_copy(v_piece(place), vbuf.at[me], v_send.at[0]),
    ] + [pltpu.make_async_copy(q_piece(place, i), qbuf[0].at[i], q_send.at[0, i]) for i in range(heads)]
    for copy in local:
        copy.start()

    @pl.when(leads)
    def _():
        send_queries()

    for r in range(group_size):
        parts[r, seq_size] = jnp.zeros((hd, rows), jnp.bfloat16)
        stats[r, seq_size, 0:1, :] = jnp.full((1, rows), LOW, jnp.float32)
        stats[r, seq_size, 1:2, :] = jnp.zeros((1, rows), jnp.float32)
    for copy in local:
        copy.wait()

    causal = lax.broadcasted_iota(jnp.int32, (rows, rows), 0) <= lax.broadcasted_iota(
        jnp.int32, (rows, rows), 1)

    def diagonal(r):
        a = base + others[r]
        keep = jnp.concatenate([causal] * heads, axis=1)
        q = jnp.concatenate([qbuf[r][i] for i in range(heads)], axis=0)
        part, top, total = attend(kbuf[a], q, vbuf[a], factor, keep)
        for i in range(heads):
            span = slice(i * rows, (i + 1) * rows)
            own_parts[r, i] = part[:, span]
            own_stats[r, i, 0:1, :] = top[:, span]
            own_stats[r, i, 1:2, :] = total[:, span]

    def selected(members, a):
        q = jnp.concatenate([qbuf[r][table[r, a]] for r in members], axis=0)
        part, top, total = attend(kbuf[a], q, vbuf[a], factor, None)
        for n, r in enumerate(members):
            span = slice(n * rows, (n + 1) * rows)
            parts[r, a] = part[:, span]
            stats[r, a, 0:1, :] = top[:, span]
            stats[r, a, 1:2, :] = total[:, span]

    def block_at(t):
        level = t // group_size
        return base - (level + 1) * group_size + member(place, t % group_size, group_size)

    def inside(r, first):
        @pl.when(others[first] < others[r])
        def _():
            selected([r], base + others[first])

    def move(t):
        for copy in relay(block_at(t)):
            copy.wait_recv()
            pl.when(has_next)(copy.start)

    diagonal(0)
    ids_own.wait()
    for r in range(1, group_size):
        ids_copy(r).wait_recv()
    ids_local = pltpu.make_async_copy(ids_in, ids, ids_sem)
    ids_local.start()
    ids_local.wait()

    picks = [(i, j) for i in range(heads) for j in range(topk)]

    def pick(r, i, j):
        return ids[r, j, 0, place * heads + i]

    def note(a, carry):
        for r in range(group_size):
            head = 0
            for i, j in picks:
                head = jnp.where(pick(r, i, j) == a, i, head)
            table[r, a] = head
        return carry

    @pl.when(trails)
    def _():
        if stagger:
            pl.semaphore_wait(kv_gate, 1)
        send_keys()

    lax.fori_loop(0, base + group_size, note, 0)

    for r in range(1, group_size):
        for copy in relay(base + others[r]):
            copy.wait_recv()
            pl.when(leads & has_next)(copy.start)

    @pl.when(leads)
    def _():
        open_gate(kv_gate)

    for r in range(1, group_size):
        inside(0, r)

    @pl.when(trails)
    def _():
        if stagger:
            pl.semaphore_wait(q_gate, 1)
        send_queries()

    @pl.when(leads & has_prev)
    def _():
        for t in range(group_size):
            move(t)

    def begin_chain():
        if stagger:
            pl.semaphore_wait(chain_gate, 1)
        for r in range(1, group_size):
            pass_on(base + others[r])

    levels_two = plane > 1

    @pl.when(leads & has_next)
    def _():
        open_gate(chain_gate)

    @pl.when(trails & has_next)
    def _():
        begin_chain()

    for r in range(1, group_size):
        for copy in sends[r][1]:
            copy.wait_recv()
        if r == 1:
            @pl.when(leads)
            def _():
                open_gate(q_gate)
        diagonal(r)

    for r in range(1, group_size):
        for first in range(group_size):
            if first != r:
                inside(r, first)

    def far(t, carry):
        selected(range(group_size), block_at(t))
        return carry

    def far_move(t, carry):
        move(t)
        return far(t, carry)

    def near(t, carry):
        @pl.when(levels_two)
        def _():
            move(t + group_size)
        return far(t, carry)

    @pl.when(leads & has_prev)
    def _():
        lax.fori_loop(0, group_size, near, 0)

    @pl.when(leads & levels_two)
    def _():
        lax.fori_loop(group_size, 2 * group_size, far, 0)
        lax.fori_loop(2 * group_size, plane * group_size, far_move, 0)

    @pl.when(trails)
    def _():
        lax.fori_loop(0, plane * group_size - 1, far_move, 0)

    def att_copy(r, i):
        return pltpu.make_async_remote_copy(
            src_ref=att_out.at[r, i], dst_ref=att_in.at[place, i], send_sem=att_send.at[r, i],
            recv_sem=att_recv.at[r, i], device_id={"seq": base + others[r]}, device_id_type=MESH)

    near_ones = [r for r in reversed(range(1, group_size)) if not r & (r - 1)]
    far_ones = [r for r in range(1, group_size) if r & (r - 1)] + [0]

    def give_back(r, i):
        block = base + others[r]
        tops = [own_stats[r, i, 0:1, :]]
        totals = [own_stats[r, i, 1:2, :]]
        slots = [jnp.where(pick(r, i, j) < block, pick(r, i, j), seq_size) for j in range(topk)]
        for slot in slots:
            tops.append(stats[r, slot, 0:1, :])
            totals.append(stats[r, slot, 1:2, :])
        top = functools.reduce(jnp.maximum, tops)
        weights = [jnp.exp2((one - top) * factor) for one in tops]
        inverse = 1.0 / sum(w * t for w, t in zip(weights, totals))
        weights = [w * inverse for w in weights]
        accum = weights[0] * own_parts[r, i].astype(jnp.float32)
        for slot, weight in zip(slots, weights[1:]):
            accum = accum + weight * parts[r, slot].astype(jnp.float32)
        attended = accum.astype(jnp.bfloat16).T
        if r:
            att_out[r, i] = attended
        else:
            att_in[place, i] = attended
        if r:
            att_copy(r, i).start()

    final = plane * group_size - 1

    @pl.when(trails & has_prev)
    def _():
        move(final)

    for members in (near_ones, far_ones):
        if members:
            @pl.when(trails & has_prev)
            def _():
                selected(members, block_at(final))

            for i in range(heads):
                for r in members:
                    give_back(r, i)

    features = w_hbm.shape[1] // head_size
    tiles = features // tile

    def product(r, start, span):
        row = pl.multiple_of(others[r] * width, width)
        rows_in = jnp.concatenate([att_in[others[r], i] for i in range(heads)], axis=1)
        return jnp.dot(
            rows_in, wbuf[pl.ds(row, width), pl.ds(start, span)],
            preferred_element_type=jnp.float32)

    w_copy.wait()

    def share(early, members):
        for r in members:
            if r:
                for i in range(heads):
                    att_copy(r, i).wait_recv()

        def one(n, carry):
            terms = [product(r, pl.multiple_of(n * tile, tile), tile) for r in members]
            acc[n] = sum(terms) if early else acc[n] + sum(terms)
            return carry

        if members:
            lax.fori_loop(0, head_size * tiles, one, 0)

    share(True, list(range(min(1, group_size - 1))))
    for r in range(1, group_size - 1):
        share(False, [r])
    if group_size > 1:
        for i in range(heads):
            att_copy(group_size - 1, i).wait_recv()

    piece = piece_out.shape[3]
    split = tile // piece

    def project(peer, n, u):
        result = product(
            group_size - 1, pl.multiple_of(peer * features + n * tile + u * piece, piece), piece)
        if group_size > 1:
            result = result + acc[peer * tiles + n][:, u * piece:(u + 1) * piece]
        return result.astype(jnp.bfloat16)

    def piece_copy(h, n):
        return pltpu.make_async_remote_copy(
            src_ref=piece_out.at[h - 1, n], dst_ref=piece_in.at[h - 1, n],
            send_sem=piece_send.at[h - 1, n], recv_sem=piece_recv.at[h - 1, n],
            device_id={"head": peers[h]}, device_id_type=MESH)

    for h in range(1, head_size):
        def give(n, carry):
            for u in range(split):
                piece_out[h - 1, n * split + u] = project(peers[h], n, u)
                piece_copy(h, n * split + u).start()
            return carry
        lax.fori_loop(0, tiles, give, 0)

    def out_copy(n):
        return pltpu.make_async_copy(out_buf.at[n], out_ref.at[n], out_sem.at[n])

    def finish(n, carry):
        for u in range(split):
            total = project(mine, n, u).astype(jnp.float32)
            for h in range(1, head_size):
                piece_copy(h, n * split + u).wait_recv()
                total = total + piece_in[h - 1, n * split + u].astype(jnp.float32)
            out_buf[n * split + u] = total.astype(jnp.bfloat16)
            out_copy(n * split + u).start()
        return carry

    lax.fori_loop(0, tiles, finish, 0)
    for n in range(tiles * split):
        out_copy(n).wait()

    for h in range(1, head_size):
        for n in range(tiles * split):
            piece_copy(h, n).wait_send()
    for r in range(1, group_size):
        ids_copy(r).wait_send()
        for i in range(heads):
            att_copy(r, i).wait_send()
        for copy in sends[r][0]:
            copy.wait_send()
        for copy in sends[r][1]:
            copy.wait_send()

    @pl.when(has_next)
    def _():
        def gone(a, carry):
            for copy in relay(a):
                copy.wait_send()
            return carry
        lax.fori_loop(0, base + group_size, gone, 0)


def flip(x_hbm, out_hbm, x_buf, out_buf, x_sem, out_sem):
    parts, rows, span = x_buf.shape
    each = x_hbm.shape[2] // span
    reads, writes = [], []
    for n in range(parts):
        reads.append(pltpu.make_async_copy(
            x_hbm.at[n // each, :, pl.ds((n % each) * span, span)], x_buf.at[n], x_sem.at[n]))
        writes.append(pltpu.make_async_copy(
            out_buf.at[n], out_hbm.at[pl.ds(n * span, span), :], out_sem.at[n]))
    for copy in reads:
        copy.start()
    for n in range(parts):
        reads[n].wait()
        out_buf[n] = x_buf[n].T
        writes[n].start()
    for copy in writes:
        copy.wait()


def local(seq_size, head_size, queries, keys, values, block_ids, out_weight):
    rows = queries.shape[0]
    hd = HEAD_DIMENSION
    kv_heads = keys.shape[1] // hd
    heads = queries.shape[1] // hd // kv_heads
    topk = block_ids.shape[2]
    model = out_weight.shape[1]
    features = model // head_size
    tile = min(1024, features)
    piece = min(512, tile)
    pieces = features // piece
    ids = jnp.transpose(block_ids, (2, 0, 1))
    bf16, f32 = jnp.bfloat16, jnp.float32
    tiles = features // tile
    dma = pltpu.SemaphoreType.DMA
    g = kv_heads
    hbm = pl.BlockSpec(memory_space=pl.ANY)
    more = max(head_size - 1, 1)
    result = pl.pallas_call(
        functools.partial(kernel, (seq_size, head_size, g, heads, topk, tile)),
        out_shape=jax.ShapeDtypeStruct((pieces, rows, piece), bf16),
        in_specs=[hbm, hbm, hbm, pl.BlockSpec(memory_space=pltpu.VMEM), hbm],
        out_specs=hbm,
        scratch_shapes=[
            pltpu.VMEM((seq_size, rows, hd), bf16),
            pltpu.VMEM((seq_size, hd, rows), bf16),
            pltpu.VMEM((g, seq_size + 1, hd, rows), bf16),
            pltpu.VMEM((g, seq_size + 1, 8, rows), f32),
            pltpu.VMEM((g, heads, hd, rows), bf16),
            pltpu.VMEM((g, heads, 8, rows), f32),
            pltpu.VMEM(out_weight.shape, bf16),
            pltpu.VMEM((g, heads, rows, hd), bf16),
            pltpu.VMEM((g, heads, rows, hd), bf16),
            pltpu.VMEM((more, pieces, rows, piece), bf16),
            pltpu.VMEM((more, pieces, rows, piece), bf16),
            pltpu.VMEM((g, hd, rows), bf16),
            pltpu.VMEM((g, *ids.shape), jnp.int32),
            pltpu.SMEM((g, *ids.shape), jnp.int32),
            pltpu.SMEM((g, seq_size), jnp.int32),
            pltpu.VMEM((head_size * tiles, rows, tile), f32),
            dma((seq_size,)), dma((seq_size,)), dma((seq_size,)), dma((seq_size,)),
            dma((g,)), dma((g,)), dma((g, heads)), dma((g, heads)),
            dma((g, heads)), dma((g, heads)), dma((more, pieces)), dma((more, pieces)), dma,
            dma((g,)), dma((g,)), dma,
        ] + [pltpu.SemaphoreType.REGULAR] * 3 + [
            pltpu.VMEM((pieces, rows, piece), bf16), dma((pieces,)),
        ] + [pltpu.VMEM((heads, rows, hd), bf16)] * g,
        compiler_params=pltpu.CompilerParams(
            collective_id=0, has_side_effects=True, vmem_limit_bytes=60 << 20),
    )(ids, queries, keys, values, out_weight)
    span = min(256, piece)
    count = features // span
    return pl.pallas_call(
        flip,
        out_shape=jax.ShapeDtypeStruct((features, rows), bf16),
        in_specs=[hbm],
        out_specs=hbm,
        scratch_shapes=[
            pltpu.VMEM((count, rows, span), bf16),
            pltpu.VMEM((count, span, rows), bf16),
            dma((count,)), dma((count,)),
        ],
    )(result)


def solution(mesh):
    return jax.shard_map(
        functools.partial(local, mesh.shape["seq"], mesh.shape["head"]),
        mesh=mesh,
        in_specs=(
            P("seq", "head"),
            P("seq", "head"),
            P("seq", "head"),
            P("seq", "head", None),
            P("head", None),
        ),
        out_specs=P("head", "seq"),
        check_vma=False,
    )
```

```python
import functools
import math

import jax
import jax.numpy as jnp
from jax import lax
from jax.experimental import pallas as pl
from jax.experimental.pallas import tpu as pltpu
from jax.sharding import PartitionSpec as P

HEAD_DIMENSION = 128
MESH = pl.DeviceIdType.MESH
LOW = -1e30


def member(position, step, size):
    if size & (size - 1):
        return lax.rem(step - position + size, size)
    other, bit = 0, 1
    while bit < size:
        digit = (position // bit) % 2
        other = other + bit * ((digit + (step // bit) % 2) % 2)
        bit *= 2
    return other


def attend(k, q, v_t, factor, keep):
    scores = lax.dot_general(k, q, (((1,), (1,)), ((), ())), preferred_element_type=jnp.float32)
    if keep is not None:
        scores = jnp.where(keep, scores, LOW)
    top = jnp.max(scores, axis=0, keepdims=True)
    prob = jnp.exp2((scores - top) * factor)
    total = jnp.sum(prob, axis=0, keepdims=True)
    part = jnp.dot(v_t, prob.astype(jnp.bfloat16), preferred_element_type=jnp.float32)
    return part.astype(jnp.bfloat16), top, total


def kernel(
    dims,
    ids_hbm, q_hbm, k_hbm, v_ref, w_hbm,
    out_ref,
    kbuf, vbuf, parts, stats, own_parts, own_stats, wbuf,
    att_out, att_in, piece_out, piece_in, v_own, ids_in, ids, table, acc,
    k_recv, v_recv, k_fwd, v_fwd, k_send, v_send, q_send, q_recv,
    att_send, att_recv, piece_send, piece_recv, w_sem,
    ids_send, ids_recv, ids_sem, kv_gate, q_gate, chain_gate, out_buf, out_sem, *qbuf,
):
    seq_size, head_size, group_size, heads, topk, tile = dims
    rows = k_hbm.shape[0]
    hd = HEAD_DIMENSION
    chains = seq_size // group_size
    width = heads * hd
    me = lax.axis_index("seq")
    mine = lax.axis_index("head")
    plane = me // group_size
    place = me % group_size
    base = plane * group_size
    factor = math.log2(math.e) / math.sqrt(hd)
    others = [member(place, r, group_size) for r in range(group_size)]
    peers = [lax.rem(mine + h, head_size) for h in range(head_size)]
    has_next = plane < chains - 1
    has_prev = plane > 0
    ahead = me + group_size
    stagger = head_size == 2 and group_size > 1
    leads = mine == 0 if stagger else mine >= 0
    trails = mine == 1 if stagger else mine < 0

    w_copy = pltpu.make_async_copy(w_hbm, wbuf, w_sem)
    w_copy.start()

    barrier = pltpu.get_barrier_semaphore()
    for r in range(1, group_size):
        pl.semaphore_signal(barrier, inc=1, device_id={"seq": base + others[r]}, device_id_type=MESH)
    for h in range(1, head_size):
        pl.semaphore_signal(barrier, inc=1, device_id={"head": peers[h]}, device_id_type=MESH)

    @pl.when(has_next)
    def _():
        pl.semaphore_signal(barrier, inc=1, device_id={"seq": ahead}, device_id_type=MESH)

    @pl.when(has_prev)
    def _():
        pl.semaphore_signal(barrier, inc=1, device_id={"seq": me - group_size}, device_id_type=MESH)

    for g in range(group_size):
        v_own[g] = v_ref[:, g * hd:(g + 1) * hd].T
    near_count = jnp.where(has_next, 1, 0) + jnp.where(has_prev, 1, 0)
    pl.semaphore_wait(barrier, group_size + head_size - 2 + near_count)

    def k_piece(head):
        return k_hbm.at[:, pl.ds(pl.multiple_of(head * hd, hd), hd)]

    def v_piece(head):
        return v_own.at[head]

    def q_piece(head, i):
        return q_hbm.at[:, pl.ds(pl.multiple_of((head * heads + i) * hd, hd), hd)]

    def forward(a, k_src, v_src):
        return (
            pltpu.make_async_remote_copy(
                src_ref=k_src, dst_ref=kbuf.at[a], send_sem=k_fwd.at[a], recv_sem=k_recv.at[a],
                device_id={"seq": ahead}, device_id_type=MESH),
            pltpu.make_async_remote_copy(
                src_ref=v_src, dst_ref=vbuf.at[a], send_sem=v_fwd.at[a], recv_sem=v_recv.at[a],
                device_id={"seq": ahead}, device_id_type=MESH),
        )

    def relay(a):
        return forward(a, kbuf.at[a], vbuf.at[a])

    def to_member(r):
        t = others[r]
        kv = (
            pltpu.make_async_remote_copy(
                src_ref=k_piece(t), dst_ref=kbuf.at[me], send_sem=k_send.at[r], recv_sem=k_recv.at[me],
                device_id={"seq": base + t}, device_id_type=MESH),
            pltpu.make_async_remote_copy(
                src_ref=v_piece(t), dst_ref=vbuf.at[me], send_sem=v_send.at[r], recv_sem=v_recv.at[me],
                device_id={"seq": base + t}, device_id_type=MESH),
        )
        qs = [
            pltpu.make_async_remote_copy(
                src_ref=q_piece(t, i), dst_ref=qbuf[r].at[i], send_sem=q_send.at[r, i],
                recv_sem=q_recv.at[r, i], device_id={"seq": base + t}, device_id_type=MESH)
            for i in range(heads)
        ]
        return kv, qs

    def ids_copy(r):
        return pltpu.make_async_remote_copy(
            src_ref=ids_hbm, dst_ref=ids_in.at[r], send_sem=ids_send.at[r],
            recv_sem=ids_recv.at[r], device_id={"seq": base + others[r]}, device_id_type=MESH)

    def pass_on(a):
        @pl.when(has_next)
        def _():
            for copy in relay(a):
                copy.start()

    def open_gate(gate):
        if stagger:
            pl.semaphore_signal(gate, inc=1, device_id={"head": peers[1]}, device_id_type=MESH)

    ids_own = pltpu.make_async_copy(ids_hbm, ids_in.at[0], ids_send.at[0])
    ids_own.start()
    for r in range(1, group_size):
        ids_copy(r).start()
    sends = [None] + [to_member(r) for r in range(1, group_size)]
    own_first = forward(me, k_piece(place), v_piece(place))

    def send_own():
        @pl.when(has_next)
        def _():
            for copy in own_first:
                copy.start()

    def send_keys():
        for r in range(1, group_size):
            for copy in sends[r][0]:
                copy.start()

    def send_queries():
        for r in range(1, group_size):
            for copy in sends[r][1]:
                copy.start()

    send_own()

    @pl.when(leads)
    def _():
        send_keys()

    local = [
        pltpu.make_async_copy(k_piece(place), kbuf.at[me], k_send.at[0]),
        pltpu.make_async_copy(v_piece(place), vbuf.at[me], v_send.at[0]),
    ] + [pltpu.make_async_copy(q_piece(place, i), qbuf[0].at[i], q_send.at[0, i]) for i in range(heads)]
    for copy in local:
        copy.start()

    @pl.when(leads)
    def _():
        send_queries()

    for r in range(group_size):
        parts[r, seq_size] = jnp.zeros((hd, rows), jnp.bfloat16)
        stats[r, seq_size, 0:1, :] = jnp.full((1, rows), LOW, jnp.float32)
        stats[r, seq_size, 1:2, :] = jnp.zeros((1, rows), jnp.float32)
    for copy in local:
        copy.wait()

    causal = lax.broadcasted_iota(jnp.int32, (rows, rows), 0) <= lax.broadcasted_iota(
        jnp.int32, (rows, rows), 1)

    def diagonal(r):
        a = base + others[r]
        keep = jnp.concatenate([causal] * heads, axis=1)
        q = jnp.concatenate([qbuf[r][i] for i in range(heads)], axis=0)
        part, top, total = attend(kbuf[a], q, vbuf[a], factor, keep)
        for i in range(heads):
            span = slice(i * rows, (i + 1) * rows)
            own_parts[r, i] = part[:, span]
            own_stats[r, i, 0:1, :] = top[:, span]
            own_stats[r, i, 1:2, :] = total[:, span]

    def selected(members, a):
        q = jnp.concatenate([qbuf[r][table[r, a]] for r in members], axis=0)
        part, top, total = attend(kbuf[a], q, vbuf[a], factor, None)
        for n, r in enumerate(members):
            span = slice(n * rows, (n + 1) * rows)
            parts[r, a] = part[:, span]
            stats[r, a, 0:1, :] = top[:, span]
            stats[r, a, 1:2, :] = total[:, span]

    def block_at(t):
        level = t // group_size
        return base - (level + 1) * group_size + member(place, t % group_size, group_size)

    def inside(r, first):
        @pl.when(others[first] < others[r])
        def _():
            selected([r], base + others[first])

    def move(t):
        for copy in relay(block_at(t)):
            copy.wait_recv()
            pl.when(has_next)(copy.start)

    diagonal(0)
    ids_own.wait()
    for r in range(1, group_size):
        ids_copy(r).wait_recv()
    ids_local = pltpu.make_async_copy(ids_in, ids, ids_sem)
    ids_local.start()
    ids_local.wait()

    picks = [(i, j) for i in range(heads) for j in range(topk)]

    def pick(r, i, j):
        return ids[r, j, 0, place * heads + i]

    def note(a, carry):
        for r in range(group_size):
            head = 0
            for i, j in picks:
                head = jnp.where(pick(r, i, j) == a, i, head)
            table[r, a] = head
        return carry

    @pl.when(trails)
    def _():
        if stagger:
            pl.semaphore_wait(kv_gate, 1)
        send_keys()

    lax.fori_loop(0, base + group_size, note, 0)

    for r in range(1, group_size):
        for copy in relay(base + others[r]):
            copy.wait_recv()
            pl.when(leads & has_next)(copy.start)

    @pl.when(leads)
    def _():
        open_gate(kv_gate)

    for r in range(1, group_size):
        inside(0, r)

    @pl.when(trails)
    def _():
        if stagger:
            pl.semaphore_wait(q_gate, 1)
        send_queries()

    @pl.when(leads & has_prev)
    def _():
        for t in range(group_size):
            move(t)

    def begin_chain():
        if stagger:
            pl.semaphore_wait(chain_gate, 1)
        for r in range(1, group_size):
            pass_on(base + others[r])

    levels_two = plane > 1

    @pl.when(leads & has_next)
    def _():
        open_gate(chain_gate)

    @pl.when(trails & has_next)
    def _():
        begin_chain()

    for r in range(1, group_size):
        for copy in sends[r][1]:
            copy.wait_recv()
        if r == 1:
            @pl.when(leads)
            def _():
                open_gate(q_gate)
        diagonal(r)

    for r in range(1, group_size):
        for first in range(group_size):
            if first != r:
                inside(r, first)

    def far(t, carry):
        selected(range(group_size), block_at(t))
        return carry

    def far_move(t, carry):
        move(t)
        return far(t, carry)

    def near(t, carry):
        @pl.when(levels_two)
        def _():
            move(t + group_size)
        return far(t, carry)

    @pl.when(leads & has_prev)
    def _():
        lax.fori_loop(0, group_size, near, 0)

    @pl.when(leads & levels_two)
    def _():
        lax.fori_loop(group_size, 2 * group_size, far, 0)
        lax.fori_loop(2 * group_size, plane * group_size, far_move, 0)

    @pl.when(trails)
    def _():
        lax.fori_loop(0, plane * group_size - 1, far_move, 0)

    def att_copy(r, i):
        return pltpu.make_async_remote_copy(
            src_ref=att_out.at[r, i], dst_ref=att_in.at[place, i], send_sem=att_send.at[r, i],
            recv_sem=att_recv.at[r, i], device_id={"seq": base + others[r]}, device_id_type=MESH)

    near_ones = [r for r in reversed(range(1, group_size)) if not r & (r - 1)]
    far_ones = [r for r in range(1, group_size) if r & (r - 1)] + [0]

    def give_back(r, i):
        block = base + others[r]
        tops = [own_stats[r, i, 0:1, :]]
        totals = [own_stats[r, i, 1:2, :]]
        slots = [jnp.where(pick(r, i, j) < block, pick(r, i, j), seq_size) for j in range(topk)]
        for slot in slots:
            tops.append(stats[r, slot, 0:1, :])
            totals.append(stats[r, slot, 1:2, :])
        top = functools.reduce(jnp.maximum, tops)
        weights = [jnp.exp2((one - top) * factor) for one in tops]
        inverse = 1.0 / sum(w * t for w, t in zip(weights, totals))
        weights = [w * inverse for w in weights]
        accum = weights[0] * own_parts[r, i].astype(jnp.float32)
        for slot, weight in zip(slots, weights[1:]):
            accum = accum + weight * parts[r, slot].astype(jnp.float32)
        attended = accum.astype(jnp.bfloat16).T
        if r:
            att_out[r, i] = attended
        else:
            att_in[place, i] = attended
        if r:
            att_copy(r, i).start()

    final = plane * group_size - 1

    @pl.when(trails & has_prev)
    def _():
        move(final)

    for members in (near_ones, far_ones):
        if members:
            @pl.when(trails & has_prev)
            def _():
                selected(members, block_at(final))

            for i in range(heads):
                for r in members:
                    give_back(r, i)

    features = w_hbm.shape[1] // head_size
    tiles = features // tile

    def product(r, start, span):
        row = pl.multiple_of(others[r] * width, width)
        rows_in = jnp.concatenate([att_in[others[r], i] for i in range(heads)], axis=1)
        return jnp.dot(
            rows_in, wbuf[pl.ds(row, width), pl.ds(start, span)],
            preferred_element_type=jnp.float32)

    w_copy.wait()

    def share(early, members):
        for r in members:
            if r:
                for i in range(heads):
                    att_copy(r, i).wait_recv()

        def one(n, carry):
            terms = [product(r, pl.multiple_of(n * tile, tile), tile) for r in members]
            acc[n] = sum(terms) if early else acc[n] + sum(terms)
            return carry

        if members:
            lax.fori_loop(0, head_size * tiles, one, 0)

    share(True, list(range(min(1, group_size - 1))))
    for r in reversed(range(1, group_size - 1)):
        share(False, [r])
    if group_size > 1:
        for i in range(heads):
            att_copy(group_size - 1, i).wait_recv()

    piece = piece_out.shape[3]
    split = tile // piece

    def project(peer, n, u):
        result = product(
            group_size - 1, pl.multiple_of(peer * features + n * tile + u * piece, piece), piece)
        if group_size > 1:
            result = result + acc[peer * tiles + n][:, u * piece:(u + 1) * piece]
        return result.astype(jnp.bfloat16)

    def piece_copy(h, n):
        return pltpu.make_async_remote_copy(
            src_ref=piece_out.at[h - 1, n], dst_ref=piece_in.at[h - 1, n],
            send_sem=piece_send.at[h - 1, n], recv_sem=piece_recv.at[h - 1, n],
            device_id={"head": peers[h]}, device_id_type=MESH)

    for h in range(1, head_size):
        def give(n, carry):
            for u in range(split):
                piece_out[h - 1, n * split + u] = project(peers[h], n, u)
                piece_copy(h, n * split + u).start()
            return carry
        lax.fori_loop(0, tiles, give, 0)

    def out_copy(n):
        return pltpu.make_async_copy(out_buf.at[n], out_ref.at[n], out_sem.at[n])

    def finish(n, carry):
        for u in range(split):
            total = project(mine, n, u).astype(jnp.float32)
            for h in range(1, head_size):
                piece_copy(h, n * split + u).wait_recv()
                total = total + piece_in[h - 1, n * split + u].astype(jnp.float32)
            out_buf[n * split + u] = total.astype(jnp.bfloat16)
            out_copy(n * split + u).start()
        return carry

    lax.fori_loop(0, tiles, finish, 0)
    for n in range(tiles * split):
        out_copy(n).wait()

    for h in range(1, head_size):
        for n in range(tiles * split):
            piece_copy(h, n).wait_send()
    for r in range(1, group_size):
        ids_copy(r).wait_send()
        for i in range(heads):
            att_copy(r, i).wait_send()
        for copy in sends[r][0]:
            copy.wait_send()
        for copy in sends[r][1]:
            copy.wait_send()

    @pl.when(has_next)
    def _():
        def gone(a, carry):
            for copy in relay(a):
                copy.wait_send()
            return carry
        lax.fori_loop(0, base + group_size, gone, 0)


def flip(x_hbm, out_hbm, x_buf, out_buf, x_sem, out_sem):
    parts, rows, span = x_buf.shape
    each = x_hbm.shape[2] // span
    reads, writes = [], []
    for n in range(parts):
        reads.append(pltpu.make_async_copy(
            x_hbm.at[n // each, :, pl.ds((n % each) * span, span)], x_buf.at[n], x_sem.at[n]))
        writes.append(pltpu.make_async_copy(
            out_buf.at[n], out_hbm.at[pl.ds(n * span, span), :], out_sem.at[n]))
    for copy in reads:
        copy.start()
    for n in range(parts):
        reads[n].wait()
        out_buf[n] = x_buf[n].T
        writes[n].start()
    for copy in writes:
        copy.wait()


def local(seq_size, head_size, queries, keys, values, block_ids, out_weight):
    rows = queries.shape[0]
    hd = HEAD_DIMENSION
    kv_heads = keys.shape[1] // hd
    heads = queries.shape[1] // hd // kv_heads
    topk = block_ids.shape[2]
    model = out_weight.shape[1]
    features = model // head_size
    tile = min(1024, features)
    piece = min(512, tile)
    pieces = features // piece
    ids = jnp.transpose(block_ids, (2, 0, 1))
    bf16, f32 = jnp.bfloat16, jnp.float32
    tiles = features // tile
    dma = pltpu.SemaphoreType.DMA
    g = kv_heads
    hbm = pl.BlockSpec(memory_space=pl.ANY)
    more = max(head_size - 1, 1)
    result = pl.pallas_call(
        functools.partial(kernel, (seq_size, head_size, g, heads, topk, tile)),
        out_shape=jax.ShapeDtypeStruct((pieces, rows, piece), bf16),
        in_specs=[hbm, hbm, hbm, pl.BlockSpec(memory_space=pltpu.VMEM), hbm],
        out_specs=hbm,
        scratch_shapes=[
            pltpu.VMEM((seq_size, rows, hd), bf16),
            pltpu.VMEM((seq_size, hd, rows), bf16),
            pltpu.VMEM((g, seq_size + 1, hd, rows), bf16),
            pltpu.VMEM((g, seq_size + 1, 8, rows), f32),
            pltpu.VMEM((g, heads, hd, rows), bf16),
            pltpu.VMEM((g, heads, 8, rows), f32),
            pltpu.VMEM(out_weight.shape, bf16),
            pltpu.VMEM((g, heads, rows, hd), bf16),
            pltpu.VMEM((g, heads, rows, hd), bf16),
            pltpu.VMEM((more, pieces, rows, piece), bf16),
            pltpu.VMEM((more, pieces, rows, piece), bf16),
            pltpu.VMEM((g, hd, rows), bf16),
            pltpu.VMEM((g, *ids.shape), jnp.int32),
            pltpu.SMEM((g, *ids.shape), jnp.int32),
            pltpu.SMEM((g, seq_size), jnp.int32),
            pltpu.VMEM((head_size * tiles, rows, tile), f32),
            dma((seq_size,)), dma((seq_size,)), dma((seq_size,)), dma((seq_size,)),
            dma((g,)), dma((g,)), dma((g, heads)), dma((g, heads)),
            dma((g, heads)), dma((g, heads)), dma((more, pieces)), dma((more, pieces)), dma,
            dma((g,)), dma((g,)), dma,
        ] + [pltpu.SemaphoreType.REGULAR] * 3 + [
            pltpu.VMEM((pieces, rows, piece), bf16), dma((pieces,)),
        ] + [pltpu.VMEM((heads, rows, hd), bf16)] * g,
        compiler_params=pltpu.CompilerParams(
            collective_id=0, has_side_effects=True, vmem_limit_bytes=60 << 20),
    )(ids, queries, keys, values, out_weight)
    span = min(256, piece)
    count = features // span
    return pl.pallas_call(
        flip,
        out_shape=jax.ShapeDtypeStruct((features, rows), bf16),
        in_specs=[hbm],
        out_specs=hbm,
        scratch_shapes=[
            pltpu.VMEM((count, rows, span), bf16),
            pltpu.VMEM((count, span, rows), bf16),
            dma((count,)), dma((count,)),
        ],
    )(result)


def solution(mesh):
    return jax.shard_map(
        functools.partial(local, mesh.shape["seq"], mesh.shape["head"]),
        mesh=mesh,
        in_specs=(
            P("seq", "head"),
            P("seq", "head"),
            P("seq", "head"),
            P("seq", "head", None),
            P("head", None),
        ),
        out_specs=P("head", "seq"),
        check_vma=False,
    )
```
